32 devices in a mesh: pair: 8 (over z, y), band: 4 (over x, core).
Axes of the slice: x: 2, y: 2, z: 4, core: 2. Of those that a mesh axis runs over, the one named last changes fastest.
Arguments:
- orbitals: bfloat16 [2048, 23, 64], P('pair'), may hold values from -6 to 6
- screening: bfloat16 [1024, 8, 1024], P('pair', None, 'band'), may hold values from -0.1875 to 0.1875
- trial: bfloat16 [1024, 23, 64], P('pair'), may hold values from -6 to 6
- pair_kpts: int32 [8, 2], replicated, may hold values from 0 to 22
- pair_q: int32 [8], replicated, may hold values from 0 to 7
Outputs:
- applied: float32 [1024, 23, 64], P('pair', None, 'band')
The draws below stay inside these ranges and needn't reach their ends.
All inputs are finite; a program needn't handle non-finite values.
Results may differ from the reference program's by a relative error of at most 0.013.
Values may be sent and summed in bfloat16 or wider, within the bound.
No kernel may reach another device: no remote copies, remote signals or barrier semaphores. Data moves between devices by JAX's collectives and lax.ppermute only.
A program may use at most 64 MiB of HBM per device.

```python
import math
import jax
import jax.numpy as jnp
import numpy as np
from jax import lax

NV = 32
NC = 32
NR = 2048
NG = 1024
KPTS = 23
Q = 8
NVEC = 64
NB = 64
NVC = 1024
PAIRS = 8


def with_ends(drawn, rng, smallest, largest):
    longest = drawn.shape.index(max(drawn.shape))
    spots = []
    for shift in (0, 1):
        where = [jax.random.randint(jax.random.fold_in(rng, axis), (), 0, length) for axis, length in enumerate(drawn.shape)]
        where[longest] = (where[longest] + shift) % drawn.shape[longest]
        spots.append(tuple(where))
    return drawn.at[spots[0]].set(smallest).at[spots[1]].set(largest)


def level_of(key, dims, split, least, high):
    factor_of, own = 1.0, jax.random.fold_in(key, 6)
    for dim, shards_of in split:
        draws = jnp.exp(jax.random.uniform(jax.random.fold_in(own, dim), (shards_of,), jnp.float32, least / len(split), high / len(split)))
        factor_of = factor_of * jnp.repeat(draws, dims[dim] // shards_of).reshape([-1 if axis == dim else 1 for axis in range(len(dims))])
    return factor_of


def rank_bounds(number_of, skew):
    loads = [(1 << 20) // math.isqrt(standing ** skew) + 1 for standing in range(1, number_of + 1)]
    spread = 1 + sum(loads) // (1 << 30)
    return np.cumsum(np.array([max(1, weight // spread) for weight in loads]))


def ranked(key, dims, number_of, skew):
    listing = rank_bounds(number_of, skew)
    ticket = jax.random.randint(jax.random.fold_in(key, 1), dims, 0, int(listing[number_of - 1]))
    rank = jnp.searchsorted(jnp.asarray(listing, jnp.int32), ticket, side="right")
    return jax.random.permutation(jax.random.fold_in(key, 2), number_of)[rank].astype(jnp.int32)


def bell_draw(key, extent, width, bound, pieces=(), held_as=jnp.bfloat16):
    result = width * jax.random.normal(key, extent, jnp.float32)
    if pieces:
        result = result * level_of(key, extent, pieces, -0.22, 0.18)
    return jnp.clip(result, -bound, bound).astype(held_as)


def setup_inputs(seed: int = 0) -> dict:
    key_of = jax.random.split(jax.random.key(seed), 6)
    return {
        "orbitals": bell_draw(key_of[0], (NR, KPTS, NB), 1.0, 6.0, ((0, 8),)),
        "screening": bell_draw(key_of[1], (NG, Q, NG), NG ** -0.5, 0.1875, ((0, 8), (2, 4))),
        "trial": bell_draw(key_of[2], (NVC, KPTS, NVEC), 1.0, 6.0, ((0, 8),)),
        "pair_kpts": with_ends(ranked(key_of[3], (PAIRS, 2), KPTS, 2), jax.random.fold_in(key_of[3], 3), 0, KPTS - 1).astype(jnp.int32),
        "pair_q": with_ends(ranked(key_of[4], (PAIRS,), Q, 1), jax.random.fold_in(key_of[4], 3), 0, Q - 1).astype(jnp.int32),
    }


def basis_rows(first_row, row_count, point_count):
    frequency = first_row + jnp.arange(row_count, dtype=jnp.int32)
    position = jnp.arange(point_count, dtype=jnp.int32)
    phase_index = (2 * position[None, :] + 1) * frequency[:, None] % (4 * point_count)
    values = jnp.cos(phase_index.astype(jnp.float32) * (math.pi / (2 * point_count))) * math.sqrt(2.0 / point_count)
    return values.astype(jnp.bfloat16)

def densities(first_set, second_set):
    merged = first_set.astype(jnp.float32)[:, :, None] * second_set.astype(jnp.float32)[:, None, :]
    return merged.reshape(first_set.shape[0], first_set.shape[1] * second_set.shape[1]).astype(jnp.bfloat16)

def transform(basis_block, first_set, second_set):
    return lax.dot_general(basis_block, densities(first_set, second_set), (((1,), (0,)), ((), ())), preferred_element_type=jnp.float32).astype(jnp.bfloat16)

def reference(orbitals, screening, trial, pair_kpts, pair_q):
    basis_full = basis_rows(0, NG, NR)
    kernel_scale = 1.0 / math.sqrt(NG)
    apply_scale = 1.0 / math.sqrt(NV * NC)

    def one_pair(output, indices):
        kpts, which_q = indices
        first_orb = lax.dynamic_index_in_dim(orbitals, kpts[0], 1, keepdims=False)
        second_orb = lax.dynamic_index_in_dim(orbitals, kpts[1], 1, keepdims=False)
        valence = transform(basis_full, first_orb[:, :NV], second_orb[:, :NV])
        conduction = transform(basis_full, first_orb[:, NV:], second_orb[:, NV:])
        screen_cols = lax.dynamic_index_in_dim(screening, which_q, 1, keepdims=False)
        screened = lax.dot_general(screen_cols, valence, (((0,), (0,)), ((), ())), preferred_element_type=jnp.float32).astype(jnp.bfloat16)
        raw = lax.dot_general(conduction, screened, (((0,), (0,)), ((), ())), preferred_element_type=jnp.float32) * kernel_scale
        kernel = raw.reshape(NC, NC, NV, NV).transpose(2, 0, 3, 1).reshape(NV * NC, NV * NC).astype(jnp.bfloat16)
        trial_first = lax.dynamic_index_in_dim(trial, kpts[0], 1, keepdims=False)
        trial_second = lax.dynamic_index_in_dim(trial, kpts[1], 1, keepdims=False)
        forward = lax.dot_general(kernel, trial_second, (((1,), (0,)), ((), ())), preferred_element_type=jnp.float32) * apply_scale
        backward = lax.dot_general(kernel, trial_first, (((0,), (0,)), ((), ())), preferred_element_type=jnp.float32) * apply_scale
        output = output.at[:, kpts[0]].add(forward)
        output = output.at[:, kpts[1]].add(backward)
        return (output, None)
    start_value = jnp.zeros((NV * NC, KPTS, NVEC), jnp.float32)
    output, ignored = lax.scan(one_pair, start_value, (pair_kpts, pair_q))
    return output
```

```python
import math

import jax
import jax.numpy as jnp
from jax import lax
from jax.experimental import pallas as pl
from jax.experimental.pallas import tpu as pltpu
from jax.sharding import Mesh, PartitionSpec as P

NV = 32
NC = 32
NR = 2048
NG = 1024
NB = 64
NVC = NV * NC
HALVES = 2
TABLE = 64
F32 = jnp.float32
BF16 = jnp.bfloat16
VMEM_LIMIT = 56 * 1024 * 1024


def dot(a, b):
    return lax.dot_general(a, b, (((1,), (0,)), ((), ())), preferred_element_type=F32)


def dot_rows(a, b):
    return lax.dot_general(a, b, (((1,), (1,)), ((), ())), preferred_element_type=F32)


def call(body, out, scratch=(), smem=0, cost=None, name=None, args=0):
    many = isinstance(out, (list, tuple))
    specs = [pl.BlockSpec(memory_space=pltpu.SMEM)] * smem + [
        pl.BlockSpec(memory_space=pltpu.VMEM)
    ] * (args - smem)
    return pl.pallas_call(
        body,
        out_shape=out,
        in_specs=specs,
        scratch_shapes=list(scratch),
        compiler_params=pltpu.CompilerParams(vmem_limit_bytes=VMEM_LIMIT),
        cost_estimate=cost,
        name=name,
    )


def cost(flops, moved):
    return pl.CostEstimate(flops=int(flops), transcendentals=0, bytes_accessed=int(moved))


def basis_kernel(out_ref, cos_low, sin_low, cos_high, sin_high):
    columns = out_ref.shape[1]
    half = columns // 2
    groups = lax.axis_size("bc")
    strip = NG // (lax.axis_size("bx") * groups)
    column = lax.broadcasted_iota(jnp.int32, (1, columns), 1)
    inner = column - half
    frequency = jnp.where(
        column < half,
        lax.axis_index("ph") * half + column,
        (inner // strip * groups + lax.axis_index("bc")) * strip + inner % strip,
    )
    period = 4 * NR
    unit = math.pi / (2 * NR)

    def angle(index):
        index = index & (period - 1)
        return jnp.where(index >= period // 2, index - period, index).astype(F32) * unit

    low = lax.broadcasted_iota(jnp.int32, (TABLE, columns), 0)
    low_angle = angle((2 * low + 1) * frequency)
    scale = math.sqrt(2.0 / NR)
    cos_low[...] = jnp.cos(low_angle) * scale
    sin_low[...] = jnp.sin(low_angle) * scale
    high = lax.broadcasted_iota(jnp.int32, (NR // TABLE, columns), 0)
    high_angle = angle(2 * TABLE * high * frequency)
    cos_high[...] = jnp.cos(high_angle)
    sin_high[...] = jnp.sin(high_angle)

    def step(block, carry):
        value = cos_low[...] * cos_high[pl.ds(block, 1), :] - sin_low[...] * sin_high[pl.ds(block, 1), :]
        out_ref[pl.ds(pl.multiple_of(block * TABLE, TABLE), TABLE), :] = value.astype(BF16)
        return carry

    lax.fori_loop(0, NR // TABLE, step, 0)


def transform_kernel(
    own_ref, other_ref, basis_ref, val_ref, cond_ref, swap_ref, first, second, density, wide
):
    side = lax.axis_index("bc")
    blocks, bands, _ = own_ref.shape
    points = NR // blocks
    for b in range(blocks):
        where = slice(b * points, (b + 1) * points)
        own = own_ref[b, :, :points].astype(F32)
        other = other_ref[b, :, :points].astype(F32)
        first[side, :, where] = own[:NV]
        second[side, :, where] = own[NV:]
        first[1 - side, :, where] = other[:NV]
        second[1 - side, :, where] = other[NV:]
    chunk = 8
    half = val_ref.shape[1]
    for kind in range(2):

        def step(i, carry):
            right = second[kind]
            for j in range(chunk):
                left = first[kind, pl.ds(i * chunk + j, 1), :]
                density[j * NV : (j + 1) * NV, :] = (left * right).astype(BF16)
            rows = pl.ds(pl.multiple_of(i * chunk * NV, chunk * NV), chunk * NV)
            result = dot(density[...], basis_ref[:, kind * half : (kind + 1) * half])
            if kind == 0:
                val_ref[rows, :] = result.astype(BF16)
            else:
                cond_ref[rows, :] = result.astype(BF16)
                for t in range(half // 128):
                    wide[t, rows, :] = result[:, t * 128 : (t + 1) * 128]
            return carry

        lax.fori_loop(0, NV // chunk, step, 0)

    def swap(d, carry):
        for t in range(half // 128):
            swap_ref[pl.ds(pl.multiple_of(d * NC, NC), NC), t * 128 : (t + 1) * 128] = wide[
                t, pl.ds(d, NC, stride=NC), :
            ].astype(BF16)
        return carry

    lax.fori_loop(0, NC, swap, 0)


def apply_kernel(
    own_ref,
    other_ref,
    val_ref,
    screen_ref,
    cond_ref,
    swap_ref,
    out_ref,
    screen,
    wide,
    screened,
    slabs,
    vectors,
    diagonal,
    sides,
):
    side = lax.axis_index("bc")
    blocks, count, width = own_ref.shape
    states = NVC // blocks
    half = val_ref.shape[1]
    strips = lax.axis_size("bx")
    tall = screen_ref.shape[1]
    broad = screen_ref.shape[2]
    for b in range(screen_ref.shape[0]):
        row, col = b // strips, b % strips
        screen[row * tall : (row + 1) * tall, col * broad : (col + 1) * broad] = screen_ref[b]
    chunk = 256

    def screen_step(i, carry):
        rows = pl.ds(pl.multiple_of(i * chunk, chunk), chunk)
        result = dot(val_ref[rows, :], screen[...])
        for t in range(half // 128):
            wide[t, rows, :] = result[:, t * 128 : (t + 1) * 128]
        screened[0, rows, :] = result.astype(BF16)
        return carry

    lax.fori_loop(0, NVC // chunk, screen_step, 0)

    def swap(w, carry):
        for t in range(half // 128):
            screened[1, pl.ds(pl.multiple_of(w * NV, NV), NV), t * 128 : (t + 1) * 128] = wide[
                t, pl.ds(w, NV, stride=NV), :
            ].astype(BF16)
        return carry

    lax.fori_loop(0, NV, swap, 0)

    repeat = 128 // NV
    lanes = repeat * count
    for b in range(blocks):
        where = slice(b * states, (b + 1) * states)
        for slot, ref in ((side, own_ref), (1 - side, other_ref)):
            turned = ref[b, :, width - states :].astype(F32).T
            vectors[slot, where, :] = jnp.concatenate([turned] * (128 // count), axis=1)
    lane = lax.broadcasted_iota(jnp.int32, (NV, lanes), 1) // count
    per = chunk // NC
    groups = NVC // 128
    total = apply_scale() * (1.0 / math.sqrt(NG))
    for kind in range(2):
        left_ref = swap_ref if kind == 0 else cond_ref

        def spread(d, carry):
            rows = vectors[1 - kind, pl.ds(d, NV, stride=NV), :]
            rows = jnp.concatenate([rows] * (lanes // 128), axis=1)
            for r in range(repeat):
                diagonal[pl.ds(pl.multiple_of(d * 128 + r * NV, NV), NV), :] = jnp.where(
                    lane == r, rows, 0.0
                ).astype(BF16)
            return carry

        lax.fori_loop(0, NC, spread, 0)

        def raw_step(i, carry):
            rows = pl.ds(pl.multiple_of(i * chunk, chunk), chunk)
            raw = dot_rows(left_ref[rows, :], screened[kind]).astype(BF16)
            for j in range(per):
                for g in range(groups):
                    slabs[i, g * NC : (g + 1) * NC, j * 128 : (j + 1) * 128] = raw[
                        j * NC : (j + 1) * NC, g * 128 : (g + 1) * 128
                    ]
            return carry

        lax.fori_loop(0, NVC // chunk, raw_step, 0)
        sides[...] = jnp.zeros_like(sides)

        def sum_step(i, carry):
            rows = pl.ds(pl.multiple_of(i * per * 128, per * 128), per * 128)
            sides[...] += dot(slabs[i], diagonal[rows, :])
            return carry

        lax.fori_loop(0, NVC // chunk, sum_step, 0)
        for g in range(groups):
            block = sides[g * NC : (g + 1) * NC, :] * total
            stacked = jnp.concatenate([block[:, r * count : (r + 1) * count] for r in range(repeat)], axis=0)
            out_ref[kind, :, g * 128 : (g + 1) * 128] = stacked.T.astype(BF16)


def apply_scale():
    return 1.0 / math.sqrt(NVC)


def gather_kernel(kpts_ref, got_ref, out_ref):
    pairs_low = lax.axis_size("bx")
    out_ref[...] = jnp.zeros_like(out_ref)
    halves, low, strips, groups = got_ref.shape[:4]
    for p in range(low * strips):
        for s in range(2):
            total = None
            for h in range(halves):
                for g in range(groups):
                    part = got_ref[h, p // strips, p % strips, g, s].astype(F32)
                    total = part if total is None else total + part
            k = kpts_ref[p, s]
            out_ref[k] += total


def on_device(orbitals, screening, trial, pair_kpts, pair_q):
    halves, low, strips, groups = (lax.axis_size(a) for a in ("ph", "pl", "bx", "bc"))
    pair_axes, all_axes = ("ph", "pl"), ("ph", "pl", "bx", "bc")
    pair_count = halves * low
    points, kpt_count, _ = orbitals.shape
    states, _, count = trial.shape
    bx, bc = lax.axis_index("bx"), lax.axis_index("bc")
    half = NG // HALVES

    near = lax.dynamic_index_in_dim(pair_kpts.reshape(low, strips, 2), bx, 1, keepdims=False)
    orbital_t = lax.dynamic_slice_in_dim(orbitals.transpose(1, 2, 0), bc * NV, NV, 1)
    orbital_part = orbital_t[near].reshape(low, 2 * NV, points)
    which = lax.dynamic_index_in_dim(near, bc, 1, keepdims=False)
    trial_part = trial.transpose(1, 2, 0)[which]
    send = jnp.concatenate([orbital_part, trial_part], axis=2)
    send = jnp.concatenate([send] * halves, axis=0)
    got = lax.all_to_all(send, pair_axes, split_axis=0, concat_axis=0, tiled=True)

    screen_send = screening.transpose(1, 0, 2)[pair_q]
    screen_got = lax.all_to_all(screen_send, ("pl", "bx"), split_axis=0, concat_axis=0, tiled=True)
    swap = [(i, i ^ 1) for i in range(groups)]
    other = lax.ppermute(got, "bc", swap)

    if points % 128 or states % 128:

        def joined(x):
            turned = x.transpose(1, 0, 2)
            return jnp.concatenate(
                [
                    turned[:, :, :points].reshape(1, x.shape[1], pair_count * points),
                    turned[:, :, points:].reshape(1, x.shape[1], pair_count * states),
                ],
                axis=2,
            )

        got, other = joined(got), joined(other)
        tall, broad = screen_got.shape[1:]
        screen_got = screen_got.reshape(low, strips, tall, broad).transpose(1, 0, 2, 3)
        screen_got = screen_got.reshape(strips, low * tall, broad)

    basis = call(
        basis_kernel,
        jax.ShapeDtypeStruct((NR, 2 * half), BF16),
        [pltpu.VMEM((TABLE, 2 * half), F32)] * 2 + [pltpu.VMEM((NR // TABLE, 2 * half), F32)] * 2,
        cost=cost(NR * NG * 4, NR * NG * 2),
        name="basis",
    )()
    valence, conduction, swapped = call(
        transform_kernel,
        [jax.ShapeDtypeStruct((NVC, half), BF16)] * 3,
        [
            pltpu.VMEM((2, NV, NR), F32),
            pltpu.VMEM((2, NV, NR), F32),
            pltpu.VMEM((8 * NV, NR), BF16),
            pltpu.VMEM((half // 128, NVC, 128), F32),
        ],
        cost=cost(2 * NVC * NR * half * 2, NR * NG * 2),
        name="transform",
        args=3,
    )(got, other, basis)
    partial = call(
        apply_kernel,
        jax.ShapeDtypeStruct((2, count, NVC), BF16),
        [
            pltpu.VMEM((half, half), BF16),
            pltpu.VMEM((half // 128, NVC, 128), F32),
            pltpu.VMEM((2, NVC, half), BF16),
            pltpu.VMEM((4, 2 * NVC // 8, 8 * 128), BF16),
            pltpu.VMEM((2, NVC, 128), F32),
            pltpu.VMEM((NC * 128, 4 * count), BF16),
            pltpu.VMEM((8 * NC, 4 * count), F32),
        ],
        cost=cost(2 * NVC * half * half + 8 * NVC * NVC * half, NVC * NVC),
        name="apply",
        args=6,
    )(got, other, valence, screen_got, conduction, swapped)

    share = count // (strips * groups)
    out_send = partial.reshape(2, strips * groups, share, pair_count, states)
    out_send = out_send.transpose(3, 1, 0, 2, 4).reshape(pair_count * strips * groups, 2, share, states)
    out_got = lax.all_to_all(out_send, all_axes, split_axis=0, concat_axis=0, tiled=True)
    out_got = out_got.reshape(halves, low, strips, groups, 2, share, states)
    if states % 128:
        summed = jnp.sum(out_got.astype(F32), axis=(0, 3)).reshape(-1, share * states)
        hot = (pair_kpts.reshape(-1)[None, :] == jnp.arange(kpt_count)[:, None]).astype(F32)
        applied = lax.dot_general(
            hot, summed, (((1,), (0,)), ((), ())), precision=lax.Precision.HIGHEST, preferred_element_type=F32
        ).reshape(kpt_count, share, states)
    else:
        applied = call(
            gather_kernel,
            jax.ShapeDtypeStruct((kpt_count, share, states), F32),
            smem=1,
            name="gather",
            args=2,
        )(pair_kpts, out_got)
    return applied.transpose(2, 0, 1)


def solution(mesh):
    pair_count, band_count = mesh.shape["pair"], mesh.shape["band"]
    shape = (HALVES, pair_count // HALVES, 2, band_count // 2)
    fine = Mesh(mesh.devices.reshape(shape), ("ph", "pl", "bx", "bc"))
    pair_axes, band_axes = ("ph", "pl"), ("bx", "bc")
    return jax.shard_map(
        on_device,
        mesh=fine,
        in_specs=(
            P(pair_axes, None, None),
            P(pair_axes, None, band_axes),
            P(pair_axes, None, None),
            P(),
            P(),
        ),
        out_specs=P(pair_axes, None, band_axes),
        check_vma=False,
    )
```

```python
import math

import jax
import jax.numpy as jnp
from jax import lax
from jax.experimental import pallas as pl
from jax.experimental.pallas import tpu as pltpu
from jax.sharding import Mesh, PartitionSpec as P

NV = 32
NC = 32
NR = 2048
NG = 1024
NVC = NV * NC
LANES = 128
HALVES = 2
TABLE = 64
F32 = jnp.float32
BF16 = jnp.bfloat16
VMEM_LIMIT = 36 * 1024 * 1024


def dot(a, b):
    return lax.dot_general(a, b, (((1,), (0,)), ((), ())), preferred_element_type=F32)


def dot_rows(a, b):
    return lax.dot_general(a, b, (((1,), (1,)), ((), ())), preferred_element_type=F32)


SPACES = {"s": pltpu.SMEM, "v": pltpu.VMEM, "h": pl.ANY}


def call(body, name, inputs, outputs, scratch=(), flops=0):
    specs, arrays = [], []
    for space, array in inputs:
        specs.append(pl.BlockSpec(memory_space=SPACES.get(space, pltpu.VMEM)))
        if space == "v":
            array = pltpu.with_memory_space_constraint(array, pltpu.VMEM)
        elif space == "h":
            array = pltpu.with_memory_space_constraint(array, pltpu.HBM)
        arrays.append(array)
    shapes, out_specs = [], []
    for space, shape, dtype in outputs:
        kind = {"v": pltpu.VMEM, "h": pltpu.HBM}.get(space, jax.ShapeDtypeStruct)
        shapes.append(kind(shape, dtype))
        out_specs.append(pl.BlockSpec(memory_space=SPACES.get(space, pltpu.VMEM)))
    return pl.pallas_call(
        body,
        out_shape=shapes,
        in_specs=specs,
        out_specs=out_specs,
        scratch_shapes=list(scratch),
        compiler_params=pltpu.CompilerParams(vmem_limit_bytes=VMEM_LIMIT),
        cost_estimate=pl.CostEstimate(flops=int(flops), transcendentals=0, bytes_accessed=1 << 20),
        name=name,
    )(*arrays)


def pack_kernel(kpts_ref, orbital_ref, trial_ref, out_ref, sems):
    bx, bc = lax.axis_index("bx"), lax.axis_index("bc")
    strips, low = lax.axis_size("bx"), lax.axis_size("pl")
    points = orbital_ref.shape[2]
    bands = pl.ds(pl.multiple_of(bc * NV, NV), NV)
    copies = []
    for d in range(out_ref.shape[0]):
        pair = d % low * strips + bx
        first, second, own = kpts_ref[0, pair], kpts_ref[1, pair], kpts_ref[bc, pair]
        for source, target in (
            (orbital_ref.at[first, bands, :], out_ref.at[d, pl.ds(0, NV), pl.ds(0, points)]),
            (orbital_ref.at[second, bands, :], out_ref.at[d, pl.ds(NV, NV), pl.ds(0, points)]),
            (trial_ref.at[own], out_ref.at[d, :, pl.ds(points, trial_ref.shape[2])]),
        ):
            copies.append(pltpu.make_async_copy(source, target, sems.at[len(copies)]))
    for copy in copies:
        copy.start()
    for copy in copies:
        copy.wait()


def make_basis(out_ref, cos_low, sin_low, cos_high, sin_high):
    columns = out_ref.shape[1]
    quarter = columns // 4
    groups = lax.axis_size("bc")
    strip = NG // (lax.axis_size("bx") * groups)
    column = lax.broadcasted_iota(jnp.int32, (1, columns), 1)
    odd = column // quarter % 2
    inner = column % quarter
    frequency = jnp.where(
        column < 2 * quarter,
        lax.axis_index("ph") * 2 * quarter + 2 * inner,
        (inner // (strip // 2) * groups + lax.axis_index("bc")) * strip + 2 * (inner % (strip // 2)),
    ) + odd
    period = 4 * NR
    unit = math.pi / (2 * NR)

    def angle(index):
        index = index & (period - 1)
        return jnp.where(index >= period // 2, index - period, index).astype(F32) * unit

    low = lax.broadcasted_iota(jnp.int32, (TABLE, columns), 0)
    low_angle = angle((2 * low + 1) * frequency)
    scale = math.sqrt(2.0 / NR)
    cos_low[...] = jnp.cos(low_angle) * scale
    sin_low[...] = jnp.sin(low_angle) * scale
    high = lax.broadcasted_iota(jnp.int32, cos_high.shape, 0)
    high_angle = angle(2 * TABLE * high * frequency)
    cos_high[...] = jnp.cos(high_angle)
    sin_high[...] = jnp.sin(high_angle)

    def step(block, carry):
        value = cos_low[...] * cos_high[pl.ds(block, 1), :] - sin_low[...] * sin_high[pl.ds(block, 1), :]
        out_ref[pl.ds(pl.multiple_of(block * TABLE, TABLE), TABLE), :] = value.astype(BF16)
        return carry

    lax.fori_loop(0, out_ref.shape[0] // TABLE, step, 0)


def prepare_kernel(q_ref, screen_ref, basis_ref, send_ref, cos_low, sin_low, cos_high, sin_high, ordered):
    make_basis(basis_ref, cos_low, sin_low, cos_high, sin_high)
    pairs, rows, columns = send_ref.shape
    kinds = screen_ref.shape[0] // rows
    source = lax.broadcasted_iota(jnp.int32, (columns, columns), 0)
    target = lax.broadcasted_iota(jnp.int32, (columns, columns), 1)
    wanted = target % (columns // 2) * 2 + target // (columns // 2)
    order = jnp.where(source == wanted, 1.0, 0.0).astype(BF16)
    result = dot(screen_ref[...], order)
    for t in range(columns // LANES):
        ordered[t] = result[:, t * LANES : (t + 1) * LANES]
    for p in range(pairs):
        q = q_ref[p]
        for odd in range(2):
            for t in range(columns // LANES):
                send_ref[p, odd * rows // 2 : (odd + 1) * rows // 2, t * LANES : (t + 1) * LANES] = ordered[
                    t, pl.ds(q + kinds * odd, rows // 2, stride=2 * kinds), :
                ].astype(BF16)


def transform_kernel(
    own_ref,
    other_ref,
    basis_ref,
    val_ref,
    cond_ref,
    swap_ref,
    diagonal_ref,
    first,
    second,
    even,
    odd,
    wide,
    vectors,
):
    side = lax.axis_index("bc")
    blocks, count, width = own_ref.shape
    points = NR // blocks
    states = NVC // blocks
    piece = 256 if points % 256 == 0 else LANES
    middle = NR // 2
    source = lax.broadcasted_iota(jnp.int32, (piece, piece), 0)
    target = lax.broadcasted_iota(jnp.int32, (piece, piece), 1)
    flip = jnp.where(source + target == piece - 1, 1.0, 0.0).astype(BF16)
    for slot, ref in ((side, own_ref), (1 - side, other_ref)):
        for start in range(0, middle, piece):
            ahead = ref[start // points, :, start % points : start % points + piece].astype(F32)
            mirror = NR - start - piece
            behind = dot(ref[mirror // points, :, mirror % points : mirror % points + piece], flip)
            for half, value in enumerate((ahead, behind)):
                first[slot, half, :, start : start + piece] = value[:NV]
                second[slot, half, :, start : start + piece] = value[NV:]
        for b in range(blocks):
            turned = ref[b, :, width - states :].astype(F32).T
            vectors[slot, b * states : (b + 1) * states, :] = jnp.concatenate([turned] * (LANES // count), axis=1)

    half = val_ref.shape[1]
    quarter = half // 2
    strips = lax.axis_size("bx")
    run = quarter // strips
    for kind in range(2):
        for v in range(NV):
            rows = slice(v * NV, (v + 1) * NV)
            ahead = first[kind, 0, v : v + 1, :] * second[kind, 0]
            behind = first[kind, 1, v : v + 1, :] * second[kind, 1]
            even[rows, :] = (ahead + behind).astype(BF16)
            odd[rows, :] = (ahead - behind).astype(BF16)
        for parity, density in enumerate((even, odd)):
            at = (2 * kind + parity) * quarter
            result = dot(density[...], basis_ref[:, at : at + quarter])
            if kind == 0:
                val_ref[:, parity * quarter : (parity + 1) * quarter] = result.astype(BF16)
            else:
                for s in range(strips):
                    part = result[:, s * run : (s + 1) * run]
                    to = (2 * s + parity) * run
                    cond_ref[:, to : to + run] = part.astype(BF16)
                    for t in range(run // LANES):
                        wide[to // LANES + t] = part[:, t * LANES : (t + 1) * LANES]
    swap_rows(wide, swap_ref)

    repeat = LANES // NV
    lanes = repeat * count
    lane = lax.broadcasted_iota(jnp.int32, (NV, lanes), 1) // count
    masks = [jnp.where(lane == r, 1.0, 0.0).astype(BF16) for r in range(repeat)]
    for kind in range(2):
        for d in range(NC):
            rows = vectors[1 - kind, pl.ds(d, NV, stride=NV), :].astype(BF16)
            rows = jnp.concatenate([rows] * (lanes // LANES), axis=1)
            for r in range(repeat):
                diagonal_ref[kind, d * LANES + r * NV : d * LANES + (r + 1) * NV, :] = rows * masks[r]


def swap_rows(wide, out_ref):
    for t in range(wide.shape[0]):
        for d in range(NC):
            out_ref[d * NC : (d + 1) * NC, t * LANES : (t + 1) * LANES] = wide[
                t, pl.ds(d, NC, stride=NC), :
            ].astype(BF16)


def apply_kernel(
    val_ref, screen_ref, cond_ref, swap_ref, diagonal_ref, out_ref, screen, wide, screened, slabs
):
    half = val_ref.shape[1]
    strips = lax.axis_size("bx")
    tall, broad = screen_ref.shape[1:]
    part = tall // 2
    for b in range(screen_ref.shape[0]):
        row, col = b // strips, b % strips
        for odd in range(2):
            at = odd * (half // 2) + row * part
            screen[at : at + part, col * broad : (col + 1) * broad] = screen_ref[b, odd * part : (odd + 1) * part]
    result = dot(val_ref[...], screen[...])
    for t in range(half // LANES):
        wide[t] = result[:, t * LANES : (t + 1) * LANES]
    screened[0] = result.astype(BF16)
    swap_rows(wide, screened.at[1])

    repeat = LANES // NV
    groups = NVC // LANES
    count = diagonal_ref.shape[2] // repeat
    scale = 1.0 / math.sqrt(NVC) / math.sqrt(NG)
    for kind in range(2):
        left_ref = swap_ref if kind == 0 else cond_ref
        raw = dot_rows(left_ref[...], screened[kind]).astype(BF16)
        for d in range(NC):
            for g in range(groups):
                slabs[kind, g * NC : (g + 1) * NC, d * LANES : (d + 1) * LANES] = raw[
                    d * NC : (d + 1) * NC, g * LANES : (g + 1) * LANES
                ]
        sides = dot(slabs[kind], diagonal_ref[kind]) * scale
        for g in range(groups):
            block = sides[g * NC : (g + 1) * NC, :]
            stacked = jnp.concatenate([block[:, r * count : (r + 1) * count] for r in range(repeat)], axis=0)
            turned = stacked.T.astype(BF16)
            if len(out_ref.shape) == 3:
                out_ref[kind, :, g * LANES : (g + 1) * LANES] = turned
            else:
                share, states = out_ref.shape[3:]
                i, at = g * LANES // states, g * LANES % states
                for b in range(out_ref.shape[1]):
                    out_ref[i, b, kind, :, at : at + LANES] = turned[b * share : (b + 1) * share]


def gather_kernel(kpts_ref, got_ref, out_ref):
    out_ref[...] = jnp.zeros_like(out_ref)
    halves, low, strips, groups = got_ref.shape[:4]
    for p in range(low * strips):
        for s in range(2):
            total = None
            for h in range(halves):
                for g in range(groups):
                    part = got_ref[h, p // strips, p % strips, g, s].astype(F32)
                    total = part if total is None else total + part
            k = kpts_ref[s, p]
            out_ref[k] += total


def table_scratch(columns, rows):
    return [pltpu.VMEM((TABLE, columns), F32)] * 2 + [pltpu.VMEM((rows // TABLE, columns), F32)] * 2


def on_device(orbitals, screening, trial, pair_kpts, pair_q):
    halves, low, strips, groups = (lax.axis_size(a) for a in ("ph", "pl", "bx", "bc"))
    pair_axes, all_axes = ("ph", "pl"), ("ph", "pl", "bx", "bc")
    pair_count = halves * low
    points, kpt_count, _ = orbitals.shape
    states, _, count = trial.shape
    tall, kinds, broad = screening.shape
    half = NG // HALVES
    aligned = points % LANES == 0 and states % LANES == 0
    orbital_t, trial_t = orbitals.transpose(1, 2, 0), trial.transpose(1, 2, 0)
    kpts_t = pair_kpts.T
    basis_out = ("v", (NR // 2, 2 * half), BF16)

    if aligned:
        send = call(
            pack_kernel,
            "pack",
            [("s", kpts_t), ("h", orbital_t), ("h", trial_t)],
            [("h", (pair_count, count, points + states), BF16)],
            [pltpu.SemaphoreType.DMA((3 * pair_count,))],
        )[0]
        basis, screen_send = call(
            prepare_kernel,
            "prepare",
            [("s", pair_q), ("b", screening.reshape(tall * kinds, broad))],
            [basis_out, ("h" if False else "b", (low * strips, tall, broad), BF16)],
            table_scratch(2 * half, NR // 2) + [pltpu.VMEM((broad // LANES, tall * kinds, LANES), F32)],
            flops=NR * NG * 4,
        )
    else:
        bx, bc = lax.axis_index("bx"), lax.axis_index("bc")
        near = lax.dynamic_index_in_dim(pair_kpts.reshape(low, strips, 2), bx, 1, keepdims=False)
        orbital_half = lax.dynamic_slice_in_dim(orbital_t, bc * NV, NV, 1)
        orbital_part = orbital_half[near].reshape(low, 2 * NV, points)
        trial_part = trial_t[lax.dynamic_index_in_dim(near, bc, 1, keepdims=False)]
        send = jnp.concatenate([orbital_part, trial_part], axis=2)
        send = jnp.concatenate([send] * halves, axis=0)
        basis = call(make_basis, "basis", [], [basis_out], table_scratch(2 * half, NR // 2), flops=NR * NG)[0]
        screen_send = screening.transpose(1, 0, 2)[pair_q]
    got = lax.all_to_all(send, pair_axes, split_axis=0, concat_axis=0, tiled=True)
    screen_got = lax.all_to_all(screen_send, ("pl", "bx"), split_axis=0, concat_axis=0, tiled=True)
    other = lax.ppermute(got, "bc", [(i, i ^ 1) for i in range(groups)])

    if not aligned:

        def joined(x):
            turned = x.transpose(1, 0, 2)
            return jnp.concatenate(
                [turned[:, :, :points].reshape(1, count, NR), turned[:, :, points:].reshape(1, count, NVC)], axis=2
            )

        got, other = joined(got), joined(other)
        screen_got = screen_got.reshape(low, strips, tall // 2, 2, broad // 2, 2).transpose(1, 3, 0, 2, 5, 4)
        screen_got = screen_got.reshape(strips, low * tall, broad)

    valence, conduction, swapped, diagonal = call(
        transform_kernel,
        "transform",
        [("v", got), ("v", other), ("v", basis)],
        [("v", (NVC, half), BF16)] * 3 + [("v", (2, NC * LANES, LANES // NV * count), BF16)],
        [
            pltpu.VMEM((2, 2, NV, NR // 2), F32),
            pltpu.VMEM((2, 2, NV, NR // 2), F32),
            pltpu.VMEM((NVC, NR // 2), BF16),
            pltpu.VMEM((NVC, NR // 2), BF16),
            pltpu.VMEM((half // LANES, NVC, LANES), F32),
            pltpu.VMEM((2, NVC, LANES), F32),
        ],
        flops=2 * NVC * NR * half,
    )
    share = count // (strips * groups)
    partial = call(
        apply_kernel,
        "apply",
        [("v", valence), ("v", screen_got), ("v", conduction), ("v", swapped), ("v", diagonal)],
        [("b", (pair_count, strips * groups, 2, share, states) if aligned else (2, count, NVC), BF16)],
        [
            pltpu.VMEM((half, half), BF16),
            pltpu.VMEM((half // LANES, NVC, LANES), F32),
            pltpu.VMEM((2, NVC, half), BF16),
            pltpu.VMEM((2, NVC // LANES * NC, NC * LANES), BF16),
        ],
        flops=2 * NVC * half * half + 8 * NVC * NVC * half,
    )[0]
    if not aligned:
        partial = partial.reshape(2, strips * groups, share, pair_count, states).transpose(3, 1, 0, 2, 4)
    out_send = partial.reshape(pair_count * strips * groups, 2, share, states)
    out_got = lax.all_to_all(out_send, all_axes, split_axis=0, concat_axis=0, tiled=True)
    out_got = out_got.reshape(halves, low, strips, groups, 2, share, states)
    if aligned:
        applied = call(
            gather_kernel,
            "gather",
            [("s", kpts_t), ("v", out_got)],
            [("b", (kpt_count, share, states), F32)],
        )[0]
    else:
        summed = jnp.sum(out_got.astype(F32), axis=(0, 3)).reshape(-1, share * states)
        hot = (pair_kpts.reshape(-1)[None, :] == jnp.arange(kpt_count)[:, None]).astype(F32)
        applied = lax.dot_general(
            hot, summed, (((1,), (0,)), ((), ())), precision=lax.Precision.HIGHEST, preferred_element_type=F32
        ).reshape(kpt_count, share, states)
    return applied.transpose(2, 0, 1)


def solution(mesh):
    pair_count, band_count = mesh.shape["pair"], mesh.shape["band"]
    shape = (HALVES, pair_count // HALVES, 2, band_count // 2)
    fine = Mesh(mesh.devices.reshape(shape), ("ph", "pl", "bx", "bc"))
    pair_axes, band_axes = ("ph", "pl"), ("bx", "bc")
    return jax.shard_map(
        on_device,
        mesh=fine,
        in_specs=(
            P(pair_axes, None, None),
            P(pair_axes, None, band_axes),
            P(pair_axes, None, None),
            P(),
            P(),
        ),
        out_specs=P(pair_axes, None, band_axes),
        check_vma=False,
    )
```

```python
import math

import jax
import jax.numpy as jnp
from jax import lax
from jax.experimental import pallas as pl
from jax.experimental.pallas import tpu as pltpu
from jax.sharding import Mesh, PartitionSpec as P

NV = 32
NC = 32
NR = 2048
NG = 1024
NVC = NV * NC
LANES = 128
HALVES = 2
TABLE = 64
F32 = jnp.float32
BF16 = jnp.bfloat16
VMEM_LIMIT = 36 * 1024 * 1024


def dot(a, b):
    return lax.dot_general(a, b, (((1,), (0,)), ((), ())), preferred_element_type=F32)


def dot_rows(a, b):
    return lax.dot_general(a, b, (((1,), (1,)), ((), ())), preferred_element_type=F32)


SPACES = {"s": pltpu.SMEM, "v": pltpu.VMEM, "h": pl.ANY}


def call(body, name, inputs, outputs, scratch=(), flops=0):
    specs, arrays = [], []
    for space, array in inputs:
        specs.append(pl.BlockSpec(memory_space=SPACES.get(space, pltpu.VMEM)))
        home = pltpu.VMEM if space == "v" else pltpu.HBM
        array = pltpu.with_memory_space_constraint(array, home)
        arrays.append(array)
    shapes, out_specs = [], []
    for space, shape, dtype in outputs:
        kind = {"v": pltpu.VMEM, "h": pltpu.HBM}.get(space, jax.ShapeDtypeStruct)
        shapes.append(kind(shape, dtype))
        out_specs.append(pl.BlockSpec(memory_space=SPACES.get(space, pltpu.VMEM)))
    return pl.pallas_call(
        body,
        out_shape=shapes,
        in_specs=specs,
        out_specs=out_specs,
        scratch_shapes=list(scratch),
        compiler_params=pltpu.CompilerParams(vmem_limit_bytes=VMEM_LIMIT),
        cost_estimate=pl.CostEstimate(flops=int(flops), transcendentals=0, bytes_accessed=1 << 20),
        name=name,
    )(*arrays)


def pack_kernel(kpts_ref, orbital_ref, trial_ref, out_ref, sems):
    bx, bc = lax.axis_index("bx"), lax.axis_index("bc")
    strips, low = lax.axis_size("bx"), lax.axis_size("pl")
    points = orbital_ref.shape[2]
    bands = pl.ds(pl.multiple_of(bc * NV, NV), NV)
    copies = []
    for d in range(out_ref.shape[0]):
        pair = d % low * strips + bx
        first, second, own = kpts_ref[0, pair], kpts_ref[1, pair], kpts_ref[bc, pair]
        for source, target in (
            (orbital_ref.at[first, bands, :], out_ref.at[d, pl.ds(0, NV), pl.ds(0, points)]),
            (orbital_ref.at[second, bands, :], out_ref.at[d, pl.ds(NV, NV), pl.ds(0, points)]),
            (trial_ref.at[own], out_ref.at[d, :, pl.ds(points, trial_ref.shape[2])]),
        ):
            copies.append(pltpu.make_async_copy(source, target, sems.at[len(copies)]))
    for copy in copies:
        copy.start()
    for copy in copies:
        copy.wait()


def make_basis(out_ref, cos_low, sin_low, cos_high, sin_high):
    columns = out_ref.shape[1]
    quarter = columns // 4
    groups = lax.axis_size("bc")
    strip = NG // (lax.axis_size("bx") * groups)
    column = lax.broadcasted_iota(jnp.int32, (1, columns), 1)
    odd = column // quarter % 2
    inner = column % quarter
    frequency = jnp.where(
        column < 2 * quarter,
        lax.axis_index("ph") * 2 * quarter + 2 * inner,
        (inner // (strip // 2) * groups + lax.axis_index("bc")) * strip + 2 * (inner % (strip // 2)),
    ) + odd
    period = 4 * NR
    unit = math.pi / (2 * NR)

    def angle(index):
        index = index & (period - 1)
        return jnp.where(index >= period // 2, index - period, index).astype(F32) * unit

    low = lax.broadcasted_iota(jnp.int32, (TABLE, columns), 0)
    low_angle = angle((2 * low + 1) * frequency)
    scale = math.sqrt(2.0 / NR)
    cos_low[...] = jnp.cos(low_angle) * scale
    sin_low[...] = jnp.sin(low_angle) * scale
    high = lax.broadcasted_iota(jnp.int32, cos_high.shape, 0)
    high_angle = angle(2 * TABLE * high * frequency)
    cos_high[...] = jnp.cos(high_angle)
    sin_high[...] = jnp.sin(high_angle)

    def step(block, carry):
        value = cos_low[...] * cos_high[pl.ds(block, 1), :] - sin_low[...] * sin_high[pl.ds(block, 1), :]
        out_ref[pl.ds(pl.multiple_of(block * TABLE, TABLE), TABLE), :] = value.astype(BF16)
        return carry

    lax.fori_loop(0, out_ref.shape[0] // TABLE, step, 0)


def prepare_kernel(q_ref, screen_ref, basis_ref, send_ref, cos_low, sin_low, cos_high, sin_high, ordered):
    make_basis(basis_ref, cos_low, sin_low, cos_high, sin_high)
    pairs, rows, columns = send_ref.shape
    kinds = screen_ref.shape[0] // rows
    source = lax.broadcasted_iota(jnp.int32, (columns, columns), 0)
    target = lax.broadcasted_iota(jnp.int32, (columns, columns), 1)
    wanted = target % (columns // 2) * 2 + target // (columns // 2)
    order = jnp.where(source == wanted, 1.0, 0.0).astype(BF16)
    result = dot(screen_ref[...], order)
    for t in range(columns // LANES):
        ordered[t] = result[:, t * LANES : (t + 1) * LANES]
    for p in range(pairs):
        q = q_ref[p]
        for odd in range(2):
            for t in range(columns // LANES):
                send_ref[p, odd * rows // 2 : (odd + 1) * rows // 2, t * LANES : (t + 1) * LANES] = ordered[
                    t, pl.ds(q + kinds * odd, rows // 2, stride=2 * kinds), :
                ].astype(BF16)


def transform_kernel(
    own_ref,
    other_ref,
    basis_ref,
    val_ref,
    cond_ref,
    swap_ref,
    diagonal_ref,
    first,
    second,
    even,
    odd,
    wide,
    vectors,
    valence,
    conduction,
    swapped,
    diagonal,
    sems,
):
    side = lax.axis_index("bc")
    blocks, count, width = own_ref.shape
    points = NR // blocks
    states = NVC // blocks
    piece = 256 if points % 256 == 0 else LANES
    middle = NR // 2
    source = lax.broadcasted_iota(jnp.int32, (piece, piece), 0)
    target = lax.broadcasted_iota(jnp.int32, (piece, piece), 1)
    flip = jnp.where(source + target == piece - 1, 1.0, 0.0).astype(BF16)
    for slot, ref in ((side, own_ref), (1 - side, other_ref)):
        for start in range(0, middle, piece):
            ahead = ref[start // points, :, start % points : start % points + piece].astype(F32)
            mirror = NR - start - piece
            behind = dot(ref[mirror // points, :, mirror % points : mirror % points + piece], flip)
            for half, value in enumerate((ahead, behind)):
                first[slot, half, :, start : start + piece] = value[:NV]
                second[slot, half, :, start : start + piece] = value[NV:]
        for b in range(blocks):
            turned = ref[b, :, width - states :].astype(F32).T
            vectors[slot, b * states : (b + 1) * states, :] = jnp.concatenate([turned] * (LANES // count), axis=1)

    copies = []
    repeat = LANES // NV
    lanes = repeat * count
    lane = lax.broadcasted_iota(jnp.int32, (NV, lanes), 1) // count
    masks = [jnp.where(lane == r, 1.0, 0.0).astype(BF16) for r in range(repeat)]
    for kind in range(2):
        for d in range(NC):
            rows = vectors[1 - kind, pl.ds(d, NV, stride=NV), :].astype(BF16)
            rows = jnp.concatenate([rows] * (lanes // LANES), axis=1)
            for r in range(repeat):
                diagonal[kind, d * LANES + r * NV : d * LANES + (r + 1) * NV, :] = rows * masks[r]

        copies.append(pltpu.make_async_copy(diagonal.at[kind], diagonal_ref.at[kind], sems.at[kind]))
        copies[-1].start()
    half = val_ref.shape[1]
    quarter = half // 2
    strips = lax.axis_size("bx")
    run = quarter // strips

    def flush(source, target):
        copies.append(pltpu.make_async_copy(source, target, sems.at[len(copies)]))
        copies[-1].start()

    for kind in (1, 0):
        for v in range(NV):
            rows = slice(v * NV, (v + 1) * NV)
            ahead = first[kind, 0, v : v + 1, :] * second[kind, 0]
            behind = first[kind, 1, v : v + 1, :] * second[kind, 1]
            even[rows, :] = (ahead + behind).astype(BF16)
            odd[rows, :] = (ahead - behind).astype(BF16)
        for parity, density in enumerate((even, odd)):
            at = (2 * kind + parity) * quarter
            result = dot(density[...], basis_ref[:, at : at + quarter])
            if kind == 0:
                valence[:, parity * quarter : (parity + 1) * quarter] = result.astype(BF16)
            else:
                for s in range(strips):
                    part = result[:, s * run : (s + 1) * run]
                    to = (2 * s + parity) * run
                    conduction[:, to : to + run] = part.astype(BF16)
                    for t in range(run // LANES):
                        wide[to // LANES + t] = part[:, t * LANES : (t + 1) * LANES]
        if kind == 1:
            flush(conduction, cond_ref)
            swap_rows(wide, swapped)
            flush(swapped, swap_ref)
    flush(valence, val_ref)
    for copy in copies:
        copy.wait()


def swap_rows(wide, out_ref):
    for t in range(wide.shape[0]):
        for d in range(NC):
            out_ref[d * NC : (d + 1) * NC, t * LANES : (t + 1) * LANES] = wide[
                t, pl.ds(d, NC, stride=NC), :
            ].astype(BF16)


def apply_kernel(
    val_ref,
    screen_ref,
    cond_ref,
    swap_ref,
    diagonal_ref,
    out_ref,
    screen,
    wide,
    screened,
    slabs,
    valence,
    conduction,
    swapped,
    diagonal,
    sems,
):
    sources = (diagonal_ref.at[0], diagonal_ref.at[1], swap_ref, cond_ref, val_ref)
    targets = (diagonal.at[0], diagonal.at[1], swapped, conduction, valence)
    copies = [pltpu.make_async_copy(a, b, sems.at[i]) for i, (a, b) in enumerate(zip(sources, targets))]
    for k in (4, 3, 1, 2, 0):
        copies[k].start()
    half = val_ref.shape[1]
    strips = lax.axis_size("bx")
    tall, broad = screen_ref.shape[1:]
    part = tall // 2
    for b in range(screen_ref.shape[0]):
        row, col = b // strips, b % strips
        for odd in range(2):
            at = odd * (half // 2) + row * part
            screen[at : at + part, col * broad : (col + 1) * broad] = screen_ref[b, odd * part : (odd + 1) * part]
    copies[4].wait()
    result = dot(valence[...], screen[...])
    for t in range(half // LANES):
        wide[t] = result[:, t * LANES : (t + 1) * LANES]
    screened[0] = result.astype(BF16)
    swap_rows(wide, screened.at[1])

    repeat = LANES // NV
    groups = NVC // LANES
    count = diagonal_ref.shape[2] // repeat
    scale = 1.0 / math.sqrt(NVC) / math.sqrt(NG)
    for kind in (1, 0):
        left_ref = swapped if kind == 0 else conduction
        copies[2 + kind].wait()
        raw = dot_rows(left_ref[...], screened[kind]).astype(BF16)
        for d in range(NC):
            for g in range(groups):
                slabs[kind, g * NC : (g + 1) * NC, d * LANES : (d + 1) * LANES] = raw[
                    d * NC : (d + 1) * NC, g * LANES : (g + 1) * LANES
                ]
        copies[kind].wait()
        sides = dot(slabs[kind], diagonal[kind]) * scale
        for g in range(groups):
            block = sides[g * NC : (g + 1) * NC, :]
            stacked = jnp.concatenate([block[:, r * count : (r + 1) * count] for r in range(repeat)], axis=0)
            turned = stacked.T.astype(BF16)
            if len(out_ref.shape) == 3:
                out_ref[kind, :, g * LANES : (g + 1) * LANES] = turned
            else:
                share, states = out_ref.shape[3:]
                i, at = g * LANES // states, g * LANES % states
                for b in range(out_ref.shape[1]):
                    out_ref[i, b, kind, :, at : at + LANES] = turned[b * share : (b + 1) * share]


def gather_kernel(kpts_ref, got_ref, out_ref):
    out_ref[...] = jnp.zeros_like(out_ref)
    halves, low, strips, groups = got_ref.shape[:4]
    for p in range(low * strips):
        for s in range(2):
            total = None
            for h in range(halves):
                for g in range(groups):
                    part = got_ref[h, p // strips, p % strips, g, s].astype(F32)
                    total = part if total is None else total + part
            k = kpts_ref[s, p]
            out_ref[k] += total


def table_scratch(columns, rows):
    return [pltpu.VMEM((TABLE, columns), F32)] * 2 + [pltpu.VMEM((rows // TABLE, columns), F32)] * 2


def on_device(orbitals, screening, trial, pair_kpts, pair_q):
    halves, low, strips, groups = (lax.axis_size(a) for a in ("ph", "pl", "bx", "bc"))
    pair_axes, all_axes = ("ph", "pl"), ("ph", "pl", "bx", "bc")
    pair_count = halves * low
    points, kpt_count, _ = orbitals.shape
    states, _, count = trial.shape
    tall, kinds, broad = screening.shape
    half = NG // HALVES
    aligned = points % LANES == 0 and states % LANES == 0
    orbital_t, trial_t = orbitals.transpose(1, 2, 0), trial.transpose(1, 2, 0)
    kpts_t = pair_kpts.T
    basis_out = ("v", (NR // 2, 2 * half), BF16)

    if aligned:
        send = call(
            pack_kernel,
            "pack",
            [("s", kpts_t), ("h", orbital_t), ("h", trial_t)],
            [("v", (pair_count, count, points + states), BF16)],
            [pltpu.SemaphoreType.DMA((3 * pair_count,))],
        )[0]
        basis, screen_send = call(
            prepare_kernel,
            "prepare",
            [("s", pair_q), ("b", screening.reshape(tall * kinds, broad))],
            [basis_out, ("v", (low * strips, tall, broad), BF16)],
            table_scratch(2 * half, NR // 2) + [pltpu.VMEM((broad // LANES, tall * kinds, LANES), F32)],
            flops=NR * NG * 4,
        )
    else:
        bx, bc = lax.axis_index("bx"), lax.axis_index("bc")
        near = lax.dynamic_index_in_dim(pair_kpts.reshape(low, strips, 2), bx, 1, keepdims=False)
        orbital_half = lax.dynamic_slice_in_dim(orbital_t, bc * NV, NV, 1)
        orbital_part = orbital_half[near].reshape(low, 2 * NV, points)
        trial_part = trial_t[lax.dynamic_index_in_dim(near, bc, 1, keepdims=False)]
        send = jnp.concatenate([orbital_part, trial_part], axis=2)
        send = jnp.concatenate([send] * halves, axis=0)
        basis = call(make_basis, "basis", [], [basis_out], table_scratch(2 * half, NR // 2), flops=NR * NG)[0]
        screen_send = screening.transpose(1, 0, 2)[pair_q]
    got = lax.all_to_all(send, pair_axes, split_axis=0, concat_axis=0, tiled=True)
    screen_got = lax.all_to_all(screen_send, ("pl", "bx"), split_axis=0, concat_axis=0, tiled=True)
    other = lax.ppermute(got, "bc", [(i, i ^ 1) for i in range(groups)])

    if not aligned:

        def joined(x):
            turned = x.transpose(1, 0, 2)
            return jnp.concatenate(
                [turned[:, :, :points].reshape(1, count, NR), turned[:, :, points:].reshape(1, count, NVC)], axis=2
            )

        got, other = joined(got), joined(other)
        screen_got = screen_got.reshape(low, strips, tall // 2, 2, broad // 2, 2).transpose(1, 3, 0, 2, 5, 4)
        screen_got = screen_got.reshape(strips, low * tall, broad)

    diagonals = (2, NC * LANES, LANES // NV * count)
    valence, conduction, swapped, diagonal = call(
        transform_kernel,
        "transform",
        [("v", got), ("v", other), ("v", basis)],
        [("h", (NVC, half), BF16)] * 3 + [("h", diagonals, BF16)],
        [
            pltpu.VMEM((2, 2, NV, NR // 2), F32),
            pltpu.VMEM((2, 2, NV, NR // 2), F32),
            pltpu.VMEM((NVC, NR // 2), BF16),
            pltpu.VMEM((NVC, NR // 2), BF16),
            pltpu.VMEM((half // LANES, NVC, LANES), F32),
            pltpu.VMEM((2, NVC, LANES), F32),
            pltpu.VMEM((NVC, half), BF16),
            pltpu.VMEM((NVC, half), BF16),
            pltpu.VMEM((NVC, half), BF16),
            pltpu.VMEM(diagonals, BF16),
            pltpu.SemaphoreType.DMA((5,)),
        ],
        flops=2 * NVC * NR * half,
    )
    share = count // (strips * groups)
    partial = call(
        apply_kernel,
        "apply",
        [("h", valence), ("v", screen_got), ("h", conduction), ("h", swapped), ("h", diagonal)],
        [("v", (pair_count, strips * groups, 2, share, states) if aligned else (2, count, NVC), BF16)],
        [
            pltpu.VMEM((half, half), BF16),
            pltpu.VMEM((half // LANES, NVC, LANES), F32),
            pltpu.VMEM((2, NVC, half), BF16),
            pltpu.VMEM((2, NVC // LANES * NC, NC * LANES), BF16),
            pltpu.VMEM((NVC, half), BF16),
            pltpu.VMEM((NVC, half), BF16),
            pltpu.VMEM((NVC, half), BF16),
            pltpu.VMEM(diagonals, BF16),
            pltpu.SemaphoreType.DMA((5,)),
        ],
        flops=2 * NVC * half * half + 8 * NVC * NVC * half,
    )[0]
    if not aligned:
        partial = partial.reshape(2, strips * groups, share, pair_count, states).transpose(3, 1, 0, 2, 4)
    out_send = partial.reshape(pair_count * strips * groups, 2, share, states)
    out_got = lax.all_to_all(out_send, all_axes, split_axis=0, concat_axis=0, tiled=True)
    out_got = out_got.reshape(halves, low, strips, groups, 2, share, states)
    if aligned:
        applied = call(
            gather_kernel,
            "gather",
            [("s", kpts_t), ("v", out_got)],
            [("b", (kpt_count, share, states), F32)],
        )[0]
    else:
        summed = jnp.sum(out_got.astype(F32), axis=(0, 3)).reshape(-1, share * states)
        hot = (pair_kpts.reshape(-1)[None, :] == jnp.arange(kpt_count)[:, None]).astype(F32)
        applied = lax.dot_general(
            hot, summed, (((1,), (0,)), ((), ())), precision=lax.Precision.HIGHEST, preferred_element_type=F32
        ).reshape(kpt_count, share, states)
    return applied.transpose(2, 0, 1)


def solution(mesh):
    pair_count, band_count = mesh.shape["pair"], mesh.shape["band"]
    shape = (HALVES, pair_count // HALVES, 2, band_count // 2)
    fine = Mesh(mesh.devices.reshape(shape), ("ph", "pl", "bx", "bc"))
    pair_axes, band_axes = ("ph", "pl"), ("bx", "bc")
    return jax.shard_map(
        on_device,
        mesh=fine,
        in_specs=(
            P(pair_axes, None, None),
            P(pair_axes, None, band_axes),
            P(pair_axes, None, None),
            P(),
            P(),
        ),
        out_specs=P(pair_axes, None, band_axes),
        check_vma=False,
    )
```

```python
import math

import jax
import jax.numpy as jnp
from jax import lax
from jax.experimental import pallas as pl
from jax.experimental.pallas import tpu as pltpu
from jax.sharding import Mesh, PartitionSpec as P


NV = 32
NC = 32
NR = 2048
NG = 1024
NVC = NV * NC
LANES = 128
HALVES = 2
TABLE = 32
F32 = jnp.float32
BF16 = jnp.bfloat16
VMEM_LIMIT = 40 * 1024 * 1024


def dot(a, b):
    return lax.dot_general(a, b, (((1,), (0,)), ((), ())), preferred_element_type=F32)


def dot_rows(a, b):
    return lax.dot_general(a, b, (((1,), (1,)), ((), ())), preferred_element_type=F32)


SPACES = {"s": pltpu.SMEM, "v": pltpu.VMEM, "h": pl.ANY}


def call(body, inputs, outputs, scratch=(), flops=0):
    specs, arrays = [], []
    for space, array in inputs:
        specs.append(pl.BlockSpec(memory_space=SPACES.get(space, pltpu.VMEM)))
        home = pltpu.VMEM if space == "v" else pltpu.HBM
        array = pltpu.with_memory_space_constraint(array, home)
        arrays.append(array)
    shapes, out_specs = [], []
    for space, shape, dtype in outputs:
        kind = {"v": pltpu.VMEM, "h": pltpu.HBM}.get(space, jax.ShapeDtypeStruct)
        shapes.append(kind(shape, dtype))
        out_specs.append(pl.BlockSpec(memory_space=SPACES.get(space, pltpu.VMEM)))
    return pl.pallas_call(
        body,
        out_shape=shapes,
        in_specs=specs,
        out_specs=out_specs,
        scratch_shapes=list(scratch),
        compiler_params=pltpu.CompilerParams(vmem_limit_bytes=VMEM_LIMIT),
        cost_estimate=pl.CostEstimate(flops=int(flops), transcendentals=0, bytes_accessed=1 << 20),
    )(*arrays)


def pack_kernel(kpts_ref, orbital_ref, trial_ref, out_ref, room, fetch_sems, send_sems):
    bx, bc = lax.axis_index("bx"), lax.axis_index("bc")
    strips, low = lax.axis_size("bx"), room.shape[0]
    points = orbital_ref.shape[2]
    bands = pl.ds(pl.multiple_of(bc * NV, NV), NV)
    fetches = []
    for d in range(low):
        pair = d * strips + bx
        first, second, own = kpts_ref[0, pair], kpts_ref[1, pair], kpts_ref[bc, pair]
        parts = (
            (orbital_ref.at[first, bands, :], room.at[d, pl.ds(0, NV), pl.ds(0, points)]),
            (orbital_ref.at[second, bands, :], room.at[d, pl.ds(NV, NV), pl.ds(0, points)]),
            (trial_ref.at[own], room.at[d, :, pl.ds(points, trial_ref.shape[2])]),
        )
        fetches.append([pltpu.make_async_copy(x, y, fetch_sems.at[d, k]) for k, (x, y) in enumerate(parts)])
        for fetch in fetches[-1]:
            fetch.start()
    sends = []
    for d in range(low):
        for fetch in fetches[d]:
            fetch.wait()
        for h in range(out_ref.shape[0] // low):
            sends.append(pltpu.make_async_copy(room.at[d], out_ref.at[h * low + d], send_sems.at[h, d]))
            sends[-1].start()
    for send in sends:
        send.wait()


def basis_kernel(out_ref, cos_low, sin_low, cos_high, sin_high, rows, sems):
    columns = rows.shape[1]
    quarter = columns // 4
    groups = lax.axis_size("bc")
    strip = NG // (lax.axis_size("bx") * groups)
    column = lax.broadcasted_iota(jnp.int32, (1, columns), 1)
    odd = column // quarter % 2
    inner = column % quarter
    frequency = jnp.where(
        column < 2 * quarter,
        lax.axis_index("ph") * 2 * quarter + 2 * inner,
        (inner // (strip // 2) * groups + lax.axis_index("bc")) * strip + 2 * (inner % (strip // 2)),
    ) + odd
    period = 4 * NR
    unit = math.pi / (2 * NR)
    fine = 8

    def turn(count, step, offset):
        multiple = lax.broadcasted_iota(jnp.int32, (count, columns), 0) * step + offset
        index = multiple * frequency & (period - 1)
        angle = jnp.where(index >= period // 2, index - period, index).astype(F32) * unit
        return jnp.cos(angle), jnp.sin(angle)

    def table(step, offset, cos_ref, sin_ref, scale):
        cos_a, sin_a = turn(fine, step, offset)
        cos_b, sin_b = turn(TABLE // fine, step * fine, 0)
        cos_a, sin_a = cos_a * scale, sin_a * scale
        for k in range(TABLE // fine):
            c, s = cos_b[k : k + 1], sin_b[k : k + 1]
            cos_ref[k * fine : (k + 1) * fine, :] = cos_a * c - sin_a * s
            sin_ref[k * fine : (k + 1) * fine, :] = sin_a * c + cos_a * s

    table(2, 1, cos_low, sin_low, math.sqrt(2.0 / NR))
    table(2 * TABLE, 0, cos_high, sin_high, 1.0)
    parts = sems.shape[0]
    blocks = rows.shape[0] // TABLE // parts
    copies = []
    for part in range(parts):

        def step(block, carry):
            high = pl.ds(block, 1)
            value = cos_low[...] * cos_high[high, :] - sin_low[...] * sin_high[high, :]
            rows[pl.ds(pl.multiple_of(block * TABLE, TABLE), TABLE), :] = value.astype(BF16)
            return carry

        lax.fori_loop(part * blocks, (part + 1) * blocks, step, 0)
        span = pl.ds(part * blocks * TABLE, blocks * TABLE)
        copies.append(pltpu.make_async_copy(rows.at[span, :], out_ref.at[span, :], sems.at[part]))
        copies[-1].start()
    for copy in copies:
        copy.wait()


def select_kernel(q_ref, screen_ref, *refs):
    sends, ordered = refs[:-1], refs[-1]
    me = lax.axis_index(("pl", "bx"))
    rows, columns = sends[0].shape
    kinds = screen_ref.shape[0] // rows
    source = lax.broadcasted_iota(jnp.int32, (columns, columns), 0)
    target = lax.broadcasted_iota(jnp.int32, (columns, columns), 1)
    wanted = target % (columns // 2) * 2 + target // (columns // 2)
    order = jnp.where(source == wanted, 1.0, 0.0).astype(BF16)
    result = dot(screen_ref[...], order)
    for t in range(columns // LANES):
        ordered[t] = result[:, t * LANES : (t + 1) * LANES]
    for distance, send in enumerate(sends):
        q = q_ref[me ^ distance]
        for odd in range(2):
            for t in range(columns // LANES):
                send[odd * rows // 2 : (odd + 1) * rows // 2, t * LANES : (t + 1) * LANES] = ordered[
                    t, pl.ds(q + kinds * odd, rows // 2, stride=2 * kinds), :
                ].astype(BF16)


def transform_kernel(
    own_ref,
    other_ref,
    basis_ref,
    val_ref,
    cond_ref,
    first,
    second,
    even,
    odd,
    basis,
    conduction,
    sems,
):
    side = lax.axis_index("bc")
    blocks, _, _ = own_ref.shape
    points = NR // blocks
    piece = 256 if points % 256 == 0 else LANES
    middle = NR // 2
    half = val_ref.shape[1]
    quarter = half // 2
    strips = lax.axis_size("bx")
    run = quarter // strips
    fetches = [
        pltpu.make_async_copy(basis_ref.at[:, pl.ds(k * half, half)], basis.at[k], sems.at[k]) for k in range(2)
    ]
    fetches[1].start()
    fetches[0].start()
    source = lax.broadcasted_iota(jnp.int32, (piece, piece), 0)
    target = lax.broadcasted_iota(jnp.int32, (piece, piece), 1)
    flip = jnp.where(source + target == piece - 1, 1.0, 0.0).astype(BF16)
    for slot, ref in ((side, own_ref), (1 - side, other_ref)):
        for start in range(0, middle, piece):
            ahead = ref[start // points, :, start % points : start % points + piece].astype(F32)
            mirror = NR - start - piece
            behind = dot(ref[mirror // points, :, mirror % points : mirror % points + piece], flip)
            for half_of, value in enumerate((ahead, behind)):
                first[slot, half_of, :, start : start + piece] = value[:NV]
                second[slot, half_of, :, start : start + piece] = value[NV:]

    store = pltpu.make_async_copy(conduction, cond_ref, sems.at[2])
    for kind in (1, 0):
        outer, inner = (second, first) if kind else (first, second)
        for v in range(NV):
            rows = slice(v * NV, (v + 1) * NV)
            ahead = outer[kind, 0, v : v + 1, :] * inner[kind, 0]
            behind = outer[kind, 1, v : v + 1, :] * inner[kind, 1]
            even[kind, rows, :] = (ahead + behind).astype(BF16)
            odd[kind, rows, :] = (ahead - behind).astype(BF16)
        fetches[kind].wait()
        for parity, density in enumerate((even, odd)):
            result = dot(density[kind], basis[kind, :, parity * quarter : (parity + 1) * quarter]).astype(BF16)
            if kind == 0:
                val_ref[:, parity * quarter : (parity + 1) * quarter] = result
            else:
                for s in range(strips):
                    to = (2 * s + parity) * run
                    conduction[:, to : to + run] = result[:, s * run : (s + 1) * run]
        if kind == 1:
            store.start()
    store.wait()


def apply_kernel(own_ref, other_ref, val_ref, cond_ref, *refs):
    *screens, out_ref, screen, screened, slabs, vectors, diagonal, conduction, sides, sem = refs
    fetch = pltpu.make_async_copy(cond_ref, conduction, sem)
    fetch.start()
    side = lax.axis_index("bc")
    blocks, count, width = own_ref.shape
    states = NVC // blocks
    half = val_ref.shape[1]
    strips = lax.axis_size("bx")
    broad = screen.shape[2]
    if len(screens) > 1:
        me = lax.axis_index(("pl", "bx"))
        part = screens[0].shape[0] // 2
        for distance, ref in enumerate(screens):
            origin = me ^ distance
            for odd in range(2):
                at = pl.multiple_of(odd * (half // 2) + origin // strips * part, part)
                screen[origin % strips, pl.ds(at, part), :] = ref[odd * part : (odd + 1) * part, :]
    else:
        screen[...] = screens[0][...]
    for s in range(strips):
        screened[:, s * broad : (s + 1) * broad] = dot(val_ref[...], screen[s]).astype(BF16)

    repeat = LANES // NV
    lanes = repeat * count
    fold = LANES // count
    lane = lax.broadcasted_iota(jnp.int32, (NV, lanes), 1) // count
    masks = [jnp.where(lane == r, 1.0, 0.0).astype(BF16) for r in range(repeat)]
    for b in range(blocks):
        for slot, ref in ((side, own_ref), (1 - side, other_ref)):
            turned = ref[b, :, width - states :].astype(F32).T
            vectors[slot, b * states : (b + 1) * states, :] = jnp.concatenate([turned] * fold, axis=1)
    groups = NVC // LANES
    scale = 1.0 / math.sqrt(NVC) / math.sqrt(NG)
    source = lax.broadcasted_iota(jnp.int32, (LANES, LANES), 0)
    target = lax.broadcasted_iota(jnp.int32, (LANES, LANES), 1)
    weave = jnp.where(target == source % NV * repeat + source // NV, 1.0, 0.0).astype(BF16)

    def put(kind, i, value):
        if len(out_ref.shape) == 3:
            out_ref[kind, :, i * LANES : (i + 1) * LANES] = value
        else:
            share, states = out_ref.shape[3:]
            to, at = i * LANES // states, i * LANES % states
            for b in range(out_ref.shape[1]):
                out_ref[to, b, kind, :, at : at + LANES] = value[b * share : (b + 1) * share]

    fetch.wait()
    for kind in range(2):
        for j in range(NC):
            rows = vectors[1, pl.ds(j, NV, stride=NV), :] if kind == 0 else vectors[0, j * NC : (j + 1) * NC, :]
            rows = jnp.concatenate([rows.astype(BF16)] * (lanes // LANES), axis=1)
            for r in range(repeat):
                diagonal[kind, j * LANES + r * NV : j * LANES + (r + 1) * NV, :] = rows * masks[r]
        left, right = (conduction, screened) if kind == 0 else (screened, conduction)
        raw = dot_rows(left[...], right[...]).astype(BF16)
        for j in range(NC):
            for g in range(groups):
                slabs[kind, g * NC : (g + 1) * NC, j * LANES : (j + 1) * LANES] = raw[
                    j * NC : (j + 1) * NC, g * LANES : (g + 1) * LANES
                ]
        total = dot(slabs[kind], diagonal[kind]) * scale
        if kind == 0:
            for g in range(groups):
                block = total[g * NC : (g + 1) * NC, :]
                stacked = jnp.concatenate([block[:, r * count : (r + 1) * count] for r in range(repeat)], axis=0)
                put(0, g, stacked.T.astype(BF16))
            continue
        for t in range(lanes // LANES):
            sides[t] = total[:, t * LANES : (t + 1) * LANES]
        for at in range(0, groups, fold):
            strands = []
            for r in range(repeat):
                for w in range(repeat):
                    pieces = [
                        sides[r // fold, pl.ds((at + f) * repeat + w, groups, stride=NV), :][
                            :, r % fold * count : (r % fold + 1) * count
                        ]
                        for f in range(fold)
                    ]
                    strands.append(jnp.concatenate(pieces, axis=1))
            stacked = jnp.concatenate(strands, axis=0).astype(BF16)
            woven = lax.dot_general(stacked, weave, (((0,), (0,)), ((), ())), preferred_element_type=F32)
            for f in range(fold):
                put(1, at + f, woven[f * count : (f + 1) * count].astype(BF16))


def gather_kernel(kpts_ref, got_ref, out_ref):
    out_ref[...] = jnp.zeros_like(out_ref)
    halves, low, strips, groups = got_ref.shape[:4]
    for p in range(low * strips):
        for s in range(2):
            total = None
            for h in range(halves):
                for g in range(groups):
                    part = got_ref[h, p // strips, p % strips, g, s].astype(F32)
                    total = part if total is None else total + part
            k = kpts_ref[s, p]
            out_ref[k] += total


def on_device(orbitals, screening, trial, pair_kpts, pair_q):
    halves, low, strips, groups = (lax.axis_size(a) for a in ("ph", "pl", "bx", "bc"))
    pair_axes, all_axes = ("ph", "pl"), ("ph", "pl", "bx", "bc")
    pair_count = halves * low
    points, kpt_count, _ = orbitals.shape
    states, _, count = trial.shape
    tall, kinds, broad = screening.shape
    half = NG // HALVES
    aligned = points % LANES == 0 and states % LANES == 0
    orbital_t, trial_t = orbitals.transpose(1, 2, 0), trial.transpose(1, 2, 0)
    kpts_t = pair_kpts.T

    if aligned:
        send = call(
            pack_kernel,
            [("s", kpts_t), ("h", orbital_t), ("h", trial_t)],
            [("h", (pair_count, count, points + states), BF16)],
            [
                pltpu.VMEM((low, count, points + states), BF16),
                pltpu.SemaphoreType.DMA((low, 3)),
                pltpu.SemaphoreType.DMA((halves, low)),
            ],
        )[0]
        screen_sends = call(
            select_kernel,
            [("s", pair_q), ("b", screening.reshape(tall * kinds, broad))],
            [("b", (tall, broad), BF16)] * (low * strips),
            [pltpu.VMEM((broad // LANES, tall * kinds, LANES), F32)],
            flops=NG * NG * 256,
        )
    else:
        bx, bc = lax.axis_index("bx"), lax.axis_index("bc")
        near = lax.dynamic_index_in_dim(pair_kpts.reshape(low, strips, 2), bx, 1, keepdims=False)
        orbital_half = lax.dynamic_slice_in_dim(orbital_t, bc * NV, NV, 1)
        orbital_part = orbital_half[near].reshape(low, 2 * NV, points)
        trial_part = trial_t[lax.dynamic_index_in_dim(near, bc, 1, keepdims=False)]
        send = jnp.concatenate([orbital_part, trial_part], axis=2)
        send = jnp.concatenate([send] * halves, axis=0)
        screen_send = screening.transpose(1, 0, 2)[pair_q]
    got = lax.all_to_all(send, pair_axes, split_axis=0, concat_axis=0, tiled=True)
    basis = call(
        basis_kernel,
        [],
        [("h", (NR // 2, 2 * half), BF16)],
        [pltpu.VMEM((TABLE, 2 * half), F32)] * 4
        + [pltpu.VMEM((NR // 2, 2 * half), BF16), pltpu.SemaphoreType.DMA((4,))],
        flops=NR * NG * 8,
    )[0]
    if aligned:
        near_axes = ("pl", "bx")
        screens = list(screen_sends[:1])
        for distance in range(1, low * strips):
            to = [(i, i ^ distance) for i in range(low * strips)]
            screens.append(lax.ppermute(screen_sends[distance], near_axes, to))
    else:
        screen_got = lax.all_to_all(screen_send, ("pl", "bx"), split_axis=0, concat_axis=0, tiled=True)
    other = lax.ppermute(got, "bc", [(i, i ^ 1) for i in range(groups)])

    if not aligned:

        def joined(x):
            turned = x.transpose(1, 0, 2)
            return jnp.concatenate(
                [turned[:, :, :points].reshape(1, count, NR), turned[:, :, points:].reshape(1, count, NVC)], axis=2
            )

        got, other = joined(got), joined(other)
        screen_got = screen_got.reshape(low, strips, tall // 2, 2, broad // 2, 2).transpose(1, 3, 0, 2, 5, 4)
        screens = [screen_got.reshape(strips, low * tall, broad)]

    valence, conduction = call(
        transform_kernel,
        [("v", got), ("v", other), ("h", basis)],
        [("v", (NVC, half), BF16), ("h", (NVC, half), BF16)],
        [
            pltpu.VMEM((2, 2, NV, NR // 2), F32),
            pltpu.VMEM((2, 2, NV, NR // 2), F32),
            pltpu.VMEM((2, NVC, NR // 2), BF16),
            pltpu.VMEM((2, NVC, NR // 2), BF16),
            pltpu.VMEM((2, NR // 2, half), BF16),
            pltpu.VMEM((NVC, half), BF16),
            pltpu.SemaphoreType.DMA((3,)),
        ],
        flops=2 * NVC * NR * half,
    )
    share = count // (strips * groups)
    lanes = LANES // NV * count
    partial = call(
        apply_kernel,
        [("v", got), ("v", other), ("v", valence), ("h", conduction)] + [("v", x) for x in screens],
        [("v", (pair_count, strips * groups, 2, share, states) if aligned else (2, count, NVC), BF16)],
        [
            pltpu.VMEM((strips, half, broad), BF16),
            pltpu.VMEM((NVC, half), BF16),
            pltpu.VMEM((2, NVC // LANES * NC, NC * LANES), BF16),
            pltpu.VMEM((2, NVC, LANES), F32),
            pltpu.VMEM((2, NC * LANES, lanes), BF16),
            pltpu.VMEM((NVC, half), BF16),
            pltpu.VMEM((lanes // LANES, NVC // LANES * NC, LANES), F32),
            pltpu.SemaphoreType.DMA,
        ],
        flops=2 * NVC * half * half + 8 * NVC * NVC * half,
    )[0]
    if not aligned:
        partial = partial.reshape(2, strips * groups, share, pair_count, states).transpose(3, 1, 0, 2, 4)
    out_send = partial.reshape(pair_count * strips * groups, 2, share, states)
    out_got = lax.all_to_all(out_send, all_axes, split_axis=0, concat_axis=0, tiled=True)
    out_got = out_got.reshape(halves, low, strips, groups, 2, share, states)
    if aligned:
        applied = call(gather_kernel, [("s", kpts_t), ("v", out_got)], [("b", (kpt_count, share, states), F32)])[0]
    else:
        summed = jnp.sum(out_got.astype(F32), axis=(0, 3)).reshape(-1, share * states)
        hot = (pair_kpts.reshape(-1)[None, :] == jnp.arange(kpt_count)[:, None]).astype(F32)
        applied = lax.dot_general(
            hot, summed, (((1,), (0,)), ((), ())), precision=lax.Precision.HIGHEST, preferred_element_type=F32
        ).reshape(kpt_count, share, states)
    return applied.transpose(2, 0, 1)


def solution(mesh):
    pair_count, band_count = mesh.shape["pair"], mesh.shape["band"]
    shape = (HALVES, pair_count // HALVES, 2, band_count // 2)
    fine = Mesh(mesh.devices.reshape(shape), ("ph", "pl", "bx", "bc"))
    pair_axes, band_axes = ("ph", "pl"), ("bx", "bc")
    return jax.shard_map(
        on_device,
        mesh=fine,
        in_specs=(
            P(pair_axes, None, None),
            P(pair_axes, None, band_axes),
            P(pair_axes, None, None),
            P(),
            P(),
        ),
        out_specs=P(pair_axes, None, band_axes),
        check_vma=False,
    )
```

```python
import math

import jax
import jax.numpy as jnp
from jax import lax
from jax.experimental import pallas as pl
from jax.experimental.pallas import tpu as pltpu
from jax.sharding import Mesh, PartitionSpec as P


NV = 32
NC = 32
NR = 2048
NG = 1024
NVC = NV * NC
LANES = 128
HALVES = 2
TABLE = 32
F32 = jnp.float32
BF16 = jnp.bfloat16
VMEM_LIMIT = 40 * 1024 * 1024


def dot(a, b):
    return lax.dot_general(a, b, (((1,), (0,)), ((), ())), preferred_element_type=F32)


def dot_rows(a, b):
    return lax.dot_general(a, b, (((1,), (1,)), ((), ())), preferred_element_type=F32)


SPACES = {"s": pltpu.SMEM, "v": pltpu.VMEM, "h": pl.ANY}


def call(body, inputs, outputs, scratch=(), flops=0):
    specs, arrays = [], []
    for space, array in inputs:
        specs.append(pl.BlockSpec(memory_space=SPACES.get(space, pltpu.VMEM)))
        home = pltpu.VMEM if space == "v" else pltpu.HBM
        array = pltpu.with_memory_space_constraint(array, home)
        arrays.append(array)
    shapes, out_specs = [], []
    for space, shape, dtype in outputs:
        kind = {"v": pltpu.VMEM, "h": pltpu.HBM}.get(space, jax.ShapeDtypeStruct)
        shapes.append(kind(shape, dtype))
        out_specs.append(pl.BlockSpec(memory_space=SPACES.get(space, pltpu.VMEM)))
    return pl.pallas_call(
        body,
        out_shape=shapes,
        in_specs=specs,
        out_specs=out_specs,
        scratch_shapes=list(scratch),
        compiler_params=pltpu.CompilerParams(vmem_limit_bytes=VMEM_LIMIT),
        cost_estimate=pl.CostEstimate(flops=int(flops), transcendentals=0, bytes_accessed=1 << 20),
    )(*arrays)


def pack_kernel(kpts_ref, q_ref, orbital_ref, trial_ref, screen_ref, out_ref, *refs):
    *sends, room, table, ordered, fetch_sems, send_sems, table_sem = refs
    bx, bc = lax.axis_index("bx"), lax.axis_index("bc")
    strips, low = lax.axis_size("bx"), room.shape[0]
    points = orbital_ref.shape[2]
    bands = pl.ds(pl.multiple_of(bc * NV, NV), NV)
    fetches = []
    for d in range(low):
        pair = d * strips + bx
        first, second, own = kpts_ref[0, pair], kpts_ref[1, pair], kpts_ref[bc, pair]
        parts = (
            (orbital_ref.at[first, bands, :], room.at[d, pl.ds(0, NV), pl.ds(0, points)]),
            (orbital_ref.at[second, bands, :], room.at[d, pl.ds(NV, NV), pl.ds(0, points)]),
            (trial_ref.at[own], room.at[d, :, pl.ds(points, trial_ref.shape[2])]),
        )
        fetches.append([pltpu.make_async_copy(x, y, fetch_sems.at[d, k]) for k, (x, y) in enumerate(parts)])
        for fetch in fetches[-1]:
            fetch.start()
    table_fetch = pltpu.make_async_copy(screen_ref, table, table_sem)
    table_fetch.start()
    copies = []
    for d in range(low):
        for fetch in fetches[d]:
            fetch.wait()
        for h in range(out_ref.shape[0] // low):
            copies.append(pltpu.make_async_copy(room.at[d], out_ref.at[h * low + d], send_sems.at[h, d]))
            copies[-1].start()
    table_fetch.wait()
    me = lax.axis_index(("pl", "bx"))
    rows, columns = sends[0].shape
    kinds = screen_ref.shape[0] // rows
    source = lax.broadcasted_iota(jnp.int32, (columns, columns), 0)
    target = lax.broadcasted_iota(jnp.int32, (columns, columns), 1)
    wanted = target % (columns // 2) * 2 + target // (columns // 2)
    order = jnp.where(source == wanted, 1.0, 0.0).astype(BF16)
    result = dot(table[...], order)
    for t in range(columns // LANES):
        ordered[t] = result[:, t * LANES : (t + 1) * LANES]
    for distance, send in zip(distances(len(sends)), sends):
        q = q_ref[me ^ own_distance(distance)]
        for odd in range(2):
            for t in range(columns // LANES):
                send[odd * rows // 2 : (odd + 1) * rows // 2, t * LANES : (t + 1) * LANES] = ordered[
                    t, pl.ds(q + kinds * odd, rows // 2, stride=2 * kinds), :
                ].astype(BF16)
    for copy in copies:
        copy.wait()


def basis_kernel(rows, cos_low, sin_low, cos_high, sin_high):
    columns = rows.shape[1]
    quarter = columns // 4
    groups = lax.axis_size("bc")
    strip = NG // (lax.axis_size("bx") * groups)
    column = lax.broadcasted_iota(jnp.int32, (1, columns), 1)
    odd = column // quarter % 2
    inner = column % quarter
    frequency = jnp.where(
        column < 2 * quarter,
        lax.axis_index("ph") * 2 * quarter + 2 * inner,
        (inner // (strip // 2) * groups + lax.axis_index("bc")) * strip + 2 * (inner % (strip // 2)),
    ) + odd
    period = 4 * NR
    unit = math.pi / (2 * NR)
    fine = 8

    def turn(count, step, offset):
        multiple = lax.broadcasted_iota(jnp.int32, (count, columns), 0) * step + offset
        index = multiple * frequency & (period - 1)
        angle = jnp.where(index >= period // 2, index - period, index).astype(F32) * unit
        return jnp.cos(angle), jnp.sin(angle)

    def table(step, offset, cos_ref, sin_ref, scale):
        cos_a, sin_a = turn(fine, step, offset)
        cos_b, sin_b = turn(TABLE // fine, step * fine, 0)
        cos_a, sin_a = cos_a * scale, sin_a * scale
        for k in range(TABLE // fine):
            c, s = cos_b[k : k + 1], sin_b[k : k + 1]
            cos_ref[k * fine : (k + 1) * fine, :] = cos_a * c - sin_a * s
            sin_ref[k * fine : (k + 1) * fine, :] = sin_a * c + cos_a * s

    table(2, 1, cos_low, sin_low, math.sqrt(2.0 / NR))
    table(2 * TABLE, 0, cos_high, sin_high, 1.0)

    def step(block, carry):
        high = pl.ds(block, 1)
        value = cos_low[...] * cos_high[high, :] - sin_low[...] * sin_high[high, :]
        rows[pl.ds(pl.multiple_of(block * TABLE, TABLE), TABLE), :] = value.astype(BF16)
        return carry

    lax.fori_loop(0, rows.shape[0] // TABLE, step, 0)


def distances(count):
    order = [0] + [d for d in (1, 7, 5, 3, 6, 4, 2) if d < count]
    order += [d for d in range(1, count) if d not in order]
    return [(d, (d << 1) % count | (d << 1) // count) for d in order]


def own_distance(pair):
    return jnp.where(lax.axis_index("bc") % 2 == 0, pair[0], pair[1])


def pair_kernel(own_ref, other_ref, basis_ref, *refs):
    *screens, out_ref, first, second, even, odd, valence, conduction, screen, screened = refs[:-4]
    slabs, vectors, diagonal, sides = refs[-4:]
    side = lax.axis_index("bc")
    blocks, count, width = own_ref.shape
    points = NR // blocks
    states = NVC // blocks
    piece = 256 if points % 256 == 0 else LANES
    middle = NR // 2
    half = valence.shape[1]
    quarter = half // 2
    strips = lax.axis_size("bx")
    run = quarter // strips
    broad = screen.shape[2]
    source = lax.broadcasted_iota(jnp.int32, (piece, piece), 0)
    target = lax.broadcasted_iota(jnp.int32, (piece, piece), 1)
    flip = jnp.where(source + target == piece - 1, 1.0, 0.0).astype(BF16)
    for slot, ref in ((side, own_ref), (1 - side, other_ref)):
        for start in range(0, middle, piece):
            ahead = ref[start // points, :, start % points : start % points + piece].astype(F32)
            mirror = NR - start - piece
            behind = dot(ref[mirror // points, :, mirror % points : mirror % points + piece], flip)
            for half_of, value in enumerate((ahead, behind)):
                first[slot, half_of, :, start : start + piece] = value[:NV]
                second[slot, half_of, :, start : start + piece] = value[NV:]

    if len(screens) > 1:
        me = lax.axis_index(("pl", "bx"))
        part = screens[0].shape[0] // 2
        for distance, ref in zip(distances(len(screens)), screens):
            origin = me ^ own_distance(distance)
            for parity in range(2):
                at = pl.multiple_of(parity * quarter + origin // strips * part, part)
                screen[origin % strips, pl.ds(at, part), :] = ref[parity * part : (parity + 1) * part, :]
    else:
        screen[...] = screens[0][...]

    repeat = LANES // NV
    lanes = repeat * count
    fold = LANES // count
    lane = lax.broadcasted_iota(jnp.int32, (NV, lanes), 1) // count
    masks = [jnp.where(lane == r, 1.0, 0.0).astype(BF16) for r in range(repeat)]
    for b in range(blocks):
        for slot, ref in ((side, own_ref), (1 - side, other_ref)):
            turned = ref[b, :, width - states :].astype(F32).T
            vectors[slot, b * states : (b + 1) * states, :] = jnp.concatenate([turned] * fold, axis=1)
    for kind in range(2):
        for j in range(NC):
            rows = vectors[1, pl.ds(j, NV, stride=NV), :] if kind == 0 else vectors[0, j * NC : (j + 1) * NC, :]
            rows = jnp.concatenate([rows.astype(BF16)] * (lanes // LANES), axis=1)
            for r in range(repeat):
                diagonal[kind, j * LANES + r * NV : j * LANES + (r + 1) * NV, :] = rows * masks[r]

    for kind in (1, 0):
        outer, inner = (second, first) if kind else (first, second)
        for v in range(NV):
            rows = slice(v * NV, (v + 1) * NV)
            ahead = outer[kind, 0, v : v + 1, :] * inner[kind, 0]
            behind = outer[kind, 1, v : v + 1, :] * inner[kind, 1]
            even[kind, rows, :] = (ahead + behind).astype(BF16)
            odd[kind, rows, :] = (ahead - behind).astype(BF16)
        for parity, density in enumerate((even, odd)):
            at = (2 * kind + parity) * quarter
            result = dot(density[kind], basis_ref[:, at : at + quarter]).astype(BF16)
            if kind == 0:
                valence[:, parity * quarter : (parity + 1) * quarter] = result
            else:
                for s in range(strips):
                    to = (2 * s + parity) * run
                    conduction[:, to : to + run] = result[:, s * run : (s + 1) * run]
    for s in range(strips):
        screened[:, s * broad : (s + 1) * broad] = dot(valence[...], screen[s]).astype(BF16)

    groups = NVC // LANES
    scale = 1.0 / math.sqrt(NVC) / math.sqrt(NG)
    source = lax.broadcasted_iota(jnp.int32, (LANES, LANES), 0)
    target = lax.broadcasted_iota(jnp.int32, (LANES, LANES), 1)
    weave = jnp.where(target == source % NV * repeat + source // NV, 1.0, 0.0).astype(BF16)

    def put(kind, i, value):
        if len(out_ref.shape) == 3:
            out_ref[kind, :, i * LANES : (i + 1) * LANES] = value
        else:
            share, states = out_ref.shape[3:]
            to, at = i * LANES // states, i * LANES % states
            for b in range(out_ref.shape[1]):
                out_ref[to, b, kind, :, at : at + LANES] = value[b * share : (b + 1) * share]

    for kind in range(2):
        left, right = (conduction, screened) if kind == 0 else (screened, conduction)
        raw = dot_rows(left[...], right[...]).astype(BF16)
        for j in range(NC):
            for g in range(groups):
                slabs[kind, g * NC : (g + 1) * NC, j * LANES : (j + 1) * LANES] = raw[
                    j * NC : (j + 1) * NC, g * LANES : (g + 1) * LANES
                ]
        total = dot(slabs[kind], diagonal[kind]) * scale
        if kind == 0:
            for g in range(groups):
                block = total[g * NC : (g + 1) * NC, :]
                stacked = jnp.concatenate([block[:, r * count : (r + 1) * count] for r in range(repeat)], axis=0)
                put(0, g, stacked.T.astype(BF16))
            continue
        for t in range(lanes // LANES):
            sides[t] = total[:, t * LANES : (t + 1) * LANES]
        for at in range(0, groups, fold):
            strands = []
            for r in range(repeat):
                for w in range(repeat):
                    pieces = [
                        sides[r // fold, pl.ds((at + f) * repeat + w, groups, stride=NV), :][
                            :, r % fold * count : (r % fold + 1) * count
                        ]
                        for f in range(fold)
                    ]
                    strands.append(jnp.concatenate(pieces, axis=1))
            stacked = jnp.concatenate(strands, axis=0).astype(BF16)
            woven = lax.dot_general(stacked, weave, (((0,), (0,)), ((), ())), preferred_element_type=F32)
            for f in range(fold):
                put(1, at + f, woven[f * count : (f + 1) * count].astype(BF16))


def gather_kernel(kpts_ref, got_ref, out_ref):
    out_ref[...] = jnp.zeros_like(out_ref)
    halves, low, strips, groups = got_ref.shape[:4]
    for p in range(low * strips):
        for s in range(2):
            total = None
            for h in range(halves):
                for g in range(groups):
                    part = got_ref[h, p // strips, p % strips, g, s].astype(F32)
                    total = part if total is None else total + part
            k = kpts_ref[s, p]
            out_ref[k] += total


def on_device(orbitals, screening, trial, pair_kpts, pair_q):
    halves, low, strips, groups = (lax.axis_size(a) for a in ("ph", "pl", "bx", "bc"))
    pair_axes, all_axes = ("ph", "pl"), ("ph", "pl", "bx", "bc")
    pair_count = halves * low
    points, kpt_count, _ = orbitals.shape
    states, _, count = trial.shape
    tall, kinds, broad = screening.shape
    half = NG // HALVES
    aligned = points % LANES == 0 and states % LANES == 0 and pair_count & (pair_count - 1) == 0
    orbital_t, trial_t = orbitals.transpose(1, 2, 0), trial.transpose(1, 2, 0)
    kpts_t = pair_kpts.T

    if aligned:
        send, *screen_sends = call(
            pack_kernel,
            [
                ("s", kpts_t),
                ("s", pair_q),
                ("h", orbital_t),
                ("h", trial_t),
                ("h", screening.reshape(tall * kinds, broad)),
            ],
            [("h", (pair_count, count, points + states), BF16)] + [("b", (tall, broad), BF16)] * (low * strips),
            [
                pltpu.VMEM((low, count, points + states), BF16),
                pltpu.VMEM((tall * kinds, broad), BF16),
                pltpu.VMEM((broad // LANES, tall * kinds, LANES), F32),
                pltpu.SemaphoreType.DMA((low, 3)),
                pltpu.SemaphoreType.DMA((halves, low)),
                pltpu.SemaphoreType.DMA,
            ],
            flops=NG * NG * 256,
        )
    else:
        bx, bc = lax.axis_index("bx"), lax.axis_index("bc")
        near = lax.dynamic_index_in_dim(pair_kpts.reshape(low, strips, 2), bx, 1, keepdims=False)
        orbital_half = lax.dynamic_slice_in_dim(orbital_t, bc * NV, NV, 1)
        orbital_part = orbital_half[near].reshape(low, 2 * NV, points)
        trial_part = trial_t[lax.dynamic_index_in_dim(near, bc, 1, keepdims=False)]
        send = jnp.concatenate([orbital_part, trial_part], axis=2)
        send = jnp.concatenate([send] * halves, axis=0)
        screen_send = screening.transpose(1, 0, 2)[pair_q]
    got = lax.all_to_all(send, pair_axes, split_axis=0, concat_axis=0, tiled=True)
    basis = call(
        basis_kernel,
        [],
        [("v", (NR // 2, 2 * half), BF16)],
        [pltpu.VMEM((TABLE, 2 * half), F32)] * 4,
        flops=NR * NG * 8,
    )[0]
    if aligned:
        screens = list(screen_sends[:1])
        for step, distance in list(enumerate(distances(low * strips)))[1:]:
            to = [
                (i * groups + g, (i ^ distance[g % 2]) * groups + g) for i in range(low * strips) for g in range(groups)
            ]
            screens.append(lax.ppermute(screen_sends[step], ("pl", "bx", "bc"), to))
    else:
        screen_got = lax.all_to_all(screen_send, ("pl", "bx"), split_axis=0, concat_axis=0, tiled=True)
    other = lax.ppermute(got, "bc", [(i, i ^ 1) for i in range(groups)])

    if not aligned:

        def joined(x):
            turned = x.transpose(1, 0, 2)
            return jnp.concatenate(
                [turned[:, :, :points].reshape(1, count, NR), turned[:, :, points:].reshape(1, count, NVC)], axis=2
            )

        got, other = joined(got), joined(other)
        screen_got = screen_got.reshape(low, strips, tall // 2, 2, broad // 2, 2).transpose(1, 3, 0, 2, 5, 4)
        screens = [screen_got.reshape(strips, low * tall, broad)]

    share = count // (strips * groups)
    lanes = LANES // NV * count
    partial = call(
        pair_kernel,
        [("v", got), ("v", other), ("v", basis)] + [("v", x) for x in screens],
        [("v", (pair_count, strips * groups, 2, share, states) if aligned else (2, count, NVC), BF16)],
        [
            pltpu.VMEM((2, 2, NV, NR // 2), F32),
            pltpu.VMEM((2, 2, NV, NR // 2), F32),
            pltpu.VMEM((2, NVC, NR // 2), BF16),
            pltpu.VMEM((2, NVC, NR // 2), BF16),
            pltpu.VMEM((NVC, half), BF16),
            pltpu.VMEM((NVC, half), BF16),
            pltpu.VMEM((strips, half, broad), BF16),
            pltpu.VMEM((NVC, half), BF16),
            pltpu.VMEM((2, NVC // LANES * NC, NC * LANES), BF16),
            pltpu.VMEM((2, NVC, LANES), F32),
            pltpu.VMEM((2, NC * LANES, lanes), BF16),
            pltpu.VMEM((lanes // LANES, NVC // LANES * NC, LANES), F32),
        ],
        flops=2 * NVC * NR * half + 2 * NVC * half * half + 8 * NVC * NVC * half,
    )[0]
    if not aligned:
        partial = partial.reshape(2, strips * groups, share, pair_count, states).transpose(3, 1, 0, 2, 4)
    out_send = partial.reshape(pair_count * strips * groups, 2, share, states)
    out_got = lax.all_to_all(out_send, all_axes, split_axis=0, concat_axis=0, tiled=True)
    out_got = out_got.reshape(halves, low, strips, groups, 2, share, states)
    if aligned:
        applied = call(gather_kernel, [("s", kpts_t), ("v", out_got)], [("b", (kpt_count, share, states), F32)])[0]
    else:
        summed = jnp.sum(out_got.astype(F32), axis=(0, 3)).reshape(-1, share * states)
        hot = (pair_kpts.reshape(-1)[None, :] == jnp.arange(kpt_count)[:, None]).astype(F32)
        applied = lax.dot_general(
            hot, summed, (((1,), (0,)), ((), ())), precision=lax.Precision.HIGHEST, preferred_element_type=F32
        ).reshape(kpt_count, share, states)
    return applied.transpose(2, 0, 1)


def solution(mesh):
    pair_count, band_count = mesh.shape["pair"], mesh.shape["band"]
    shape = (HALVES, pair_count // HALVES, 2, band_count // 2)
    fine = Mesh(mesh.devices.reshape(shape), ("ph", "pl", "bx", "bc"))
    pair_axes, band_axes = ("ph", "pl"), ("bx", "bc")
    return jax.shard_map(
        on_device,
        mesh=fine,
        in_specs=(
            P(pair_axes, None, None),
            P(pair_axes, None, band_axes),
            P(pair_axes, None, None),
            P(),
            P(),
        ),
        out_specs=P(pair_axes, None, band_axes),
        check_vma=False,
    )
```

```python
import math

import jax
import jax.numpy as jnp
from jax import lax
from jax.experimental import pallas as pl
from jax.experimental.pallas import tpu as pltpu
from jax.sharding import Mesh, PartitionSpec as P


NV = 32
NC = 32
NR = 2048
NG = 1024
NVC = NV * NC
LANES = 128
HALVES = 2
TABLE = 32
F32 = jnp.float32
BF16 = jnp.bfloat16
VMEM_LIMIT = 40 * 1024 * 1024


def dot(a, b):
    return lax.dot_general(a, b, (((1,), (0,)), ((), ())), preferred_element_type=F32)


def dot_rows(a, b):
    return lax.dot_general(a, b, (((1,), (1,)), ((), ())), preferred_element_type=F32)


SPACES = {"s": pltpu.SMEM, "v": pltpu.VMEM, "h": pl.ANY}


def call(body, inputs, outputs, scratch=(), flops=0, aliases=None):
    specs, arrays = [], []
    for space, array in inputs:
        specs.append(pl.BlockSpec(memory_space=SPACES.get(space, pltpu.VMEM)))
        home = pltpu.VMEM if space == "v" else pltpu.HBM
        array = pltpu.with_memory_space_constraint(array, home)
        arrays.append(array)
    shapes, out_specs = [], []
    for space, shape, dtype in outputs:
        kind = {"v": pltpu.VMEM, "h": pltpu.HBM}.get(space, jax.ShapeDtypeStruct)
        shapes.append(kind(shape, dtype))
        out_specs.append(pl.BlockSpec(memory_space=SPACES.get(space, pltpu.VMEM)))
    return pl.pallas_call(
        body,
        out_shape=shapes,
        in_specs=specs,
        out_specs=out_specs,
        scratch_shapes=list(scratch),
        input_output_aliases=aliases or {},
        compiler_params=pltpu.CompilerParams(vmem_limit_bytes=VMEM_LIMIT),
        cost_estimate=pl.CostEstimate(flops=int(flops), transcendentals=0, bytes_accessed=1 << 20),
    )(*arrays)


def pack_kernel(kpts_ref, q_ref, orbital_ref, trial_ref, screen_ref, out_ref, *refs):
    *sends, room, table, ordered, fetch_sems, send_sems, table_sem = refs
    bx, bc = lax.axis_index("bx"), lax.axis_index("bc")
    strips, low = lax.axis_size("bx"), room.shape[0]
    points = orbital_ref.shape[2]
    bands = pl.ds(pl.multiple_of(bc * NV, NV), NV)
    fetches = []
    for d in range(low):
        pair = d * strips + bx
        first, second, own = kpts_ref[0, pair], kpts_ref[1, pair], kpts_ref[bc, pair]
        parts = (
            (orbital_ref.at[first, bands, :], room.at[d, pl.ds(0, NV), pl.ds(0, points)]),
            (orbital_ref.at[second, bands, :], room.at[d, pl.ds(NV, NV), pl.ds(0, points)]),
            (trial_ref.at[own], room.at[d, :, pl.ds(points, trial_ref.shape[2])]),
        )
        fetches.append([pltpu.make_async_copy(x, y, fetch_sems.at[d, k]) for k, (x, y) in enumerate(parts)])
        for fetch in fetches[-1]:
            fetch.start()
    table_fetch = pltpu.make_async_copy(screen_ref, table, table_sem)
    table_fetch.start()
    copies = []
    for d in range(low):
        for fetch in fetches[d]:
            fetch.wait()
        for h in range(out_ref.shape[0] // low):
            copies.append(pltpu.make_async_copy(room.at[d], out_ref.at[h * low + d], send_sems.at[h, d]))
            copies[-1].start()
    table_fetch.wait()
    me = lax.axis_index(("pl", "bx"))
    rows, columns = sends[0].shape
    kinds = screen_ref.shape[0] // rows
    source = lax.broadcasted_iota(jnp.int32, (columns, columns), 0)
    target = lax.broadcasted_iota(jnp.int32, (columns, columns), 1)
    wanted = target % (columns // 2) * 2 + target // (columns // 2)
    order = jnp.where(source == wanted, 1.0, 0.0).astype(BF16)
    result = dot(table[...], order)
    for t in range(columns // LANES):
        ordered[t] = result[:, t * LANES : (t + 1) * LANES]
    for distance, send in zip(distances(len(sends)), sends):
        q = q_ref[me ^ own_distance(distance)]
        for odd in range(2):
            for t in range(columns // LANES):
                send[odd * rows // 2 : (odd + 1) * rows // 2, t * LANES : (t + 1) * LANES] = ordered[
                    t, pl.ds(q + kinds * odd, rows // 2, stride=2 * kinds), :
                ].astype(BF16)
    for copy in copies:
        copy.wait()


def basis_kernel(rows, cos_low, sin_low, cos_high, sin_high):
    columns = rows.shape[1]
    quarter = columns // 4
    groups = lax.axis_size("bc")
    strip = NG // (lax.axis_size("bx") * groups)
    column = lax.broadcasted_iota(jnp.int32, (1, columns), 1)
    odd = column // quarter % 2
    inner = column % quarter
    frequency = jnp.where(
        column < 2 * quarter,
        lax.axis_index("ph") * 2 * quarter + 2 * inner,
        (inner // (strip // 2) * groups + lax.axis_index("bc")) * strip + 2 * (inner % (strip // 2)),
    ) + odd
    period = 4 * NR
    unit = math.pi / (2 * NR)
    fine = 8

    def turn(count, step, offset):
        multiple = lax.broadcasted_iota(jnp.int32, (count, columns), 0) * step + offset
        index = multiple * frequency & (period - 1)
        angle = jnp.where(index >= period // 2, index - period, index).astype(F32) * unit
        return jnp.cos(angle), jnp.sin(angle)

    def table(step, offset, cos_ref, sin_ref, scale):
        cos_a, sin_a = turn(fine, step, offset)
        cos_b, sin_b = turn(TABLE // fine, step * fine, 0)
        cos_a, sin_a = cos_a * scale, sin_a * scale
        for k in range(TABLE // fine):
            c, s = cos_b[k : k + 1], sin_b[k : k + 1]
            cos_ref[k * fine : (k + 1) * fine, :] = cos_a * c - sin_a * s
            sin_ref[k * fine : (k + 1) * fine, :] = sin_a * c + cos_a * s

    table(2, 1, cos_low, sin_low, math.sqrt(2.0 / NR))
    table(2 * TABLE, 0, cos_high, sin_high, 1.0)

    def step(block, carry):
        high = pl.ds(block, 1)
        value = cos_low[...] * cos_high[high, :] - sin_low[...] * sin_high[high, :]
        rows[pl.ds(pl.multiple_of(block * TABLE, TABLE), TABLE), :] = value.astype(BF16)
        return carry

    lax.fori_loop(0, rows.shape[0] // TABLE, step, 0)


def distances(count):
    order = [0] + [d for d in (1, 7, 5, 3, 6, 4, 2) if d < count]
    order += [d for d in range(1, count) if d not in order]
    return [(d, (d << 1) % count | (d << 1) // count) for d in order]


def own_distance(pair):
    return jnp.where(lax.axis_index("bc") % 2 == 0, pair[0], pair[1])


def waves_kernel(own_ref, other_ref, _, waves_ref, first, second, even, odd):
    side = lax.axis_index("bc")
    blocks, _, _ = own_ref.shape
    points = NR // blocks
    piece = 256 if points % 256 == 0 else LANES
    middle = NR // 2
    quarter = waves_ref.shape[1] // 4
    source = lax.broadcasted_iota(jnp.int32, (piece, piece), 0)
    target = lax.broadcasted_iota(jnp.int32, (piece, piece), 1)
    flip = jnp.where(source + target == piece - 1, 1.0, 0.0).astype(BF16)
    for slot, ref in ((side, own_ref), (1 - side, other_ref)):
        for start in range(0, middle, piece):
            ahead = ref[start // points, :, start % points : start % points + piece].astype(F32)
            mirror = NR - start - piece
            behind = dot(ref[mirror // points, :, mirror % points : mirror % points + piece], flip)
            for half_of, value in enumerate((ahead, behind)):
                first[slot, half_of, :, start : start + piece] = value[:NV]
                second[slot, half_of, :, start : start + piece] = value[NV:]

    for kind in (1, 0):
        outer, inner = (second, first) if kind else (first, second)
        for v in range(NV):
            rows = slice(v * NV, (v + 1) * NV)
            ahead = outer[kind, 0, v : v + 1, :] * inner[kind, 0]
            behind = outer[kind, 1, v : v + 1, :] * inner[kind, 1]
            even[kind, rows, :] = (ahead + behind).astype(BF16)
            odd[kind, rows, :] = (ahead - behind).astype(BF16)
        spans = [slice((2 * kind + parity) * quarter, (2 * kind + parity + 1) * quarter) for parity in range(2)]
        results = [dot(x[kind], waves_ref[:, span]).astype(BF16) for x, span in zip((even, odd), spans)]
        for span, result in zip(spans, results):
            waves_ref[:, span] = result


def pair_kernel(own_ref, other_ref, waves_ref, *refs):
    *screens, keep_ref, give_ref, conduction, screen, screened = refs[:-5]
    slabs, vectors, diagonal, sides, shares = refs[-5:]
    side = lax.axis_index("bc")
    blocks, count, width = own_ref.shape
    states = NVC // blocks
    half = screened.shape[1]
    quarter = half // 2
    strips = lax.axis_size("bx")
    run = quarter // strips
    broad = screen.shape[2]
    for parity in range(2):
        for s in range(strips):
            source, target = half + parity * quarter + s * run, (2 * s + parity) * run
            conduction[:, target : target + run] = waves_ref[:, source : source + run]
    if len(screens) > 1:
        me = lax.axis_index(("pl", "bx"))
        part = screens[0].shape[0] // 2
        for distance, ref in zip(distances(len(screens)), screens):
            origin = me ^ own_distance(distance)
            for parity in range(2):
                at = pl.multiple_of(parity * quarter + origin // strips * part, part)
                screen[origin % strips, pl.ds(at, part), :] = ref[parity * part : (parity + 1) * part, :]
    else:
        screen[...] = screens[0][...]

    repeat = LANES // NV
    lanes = repeat * count
    fold = LANES // count
    lane = lax.broadcasted_iota(jnp.int32, (NV, lanes), 1) // count
    masks = [jnp.where(lane == r, 1.0, 0.0).astype(BF16) for r in range(repeat)]
    for b in range(blocks):
        for slot, ref in ((side, own_ref), (1 - side, other_ref)):
            turned = ref[b, :, width - states :].astype(F32).T
            vectors[slot, b * states : (b + 1) * states, :] = jnp.concatenate([turned] * fold, axis=1)
    for kind in range(2):
        for j in range(NC):
            rows = vectors[1, pl.ds(j, NV, stride=NV), :] if kind == 0 else vectors[0, j * NC : (j + 1) * NC, :]
            rows = jnp.concatenate([rows.astype(BF16)] * (lanes // LANES), axis=1)
            for r in range(repeat):
                diagonal[kind, j * LANES + r * NV : j * LANES + (r + 1) * NV, :] = rows * masks[r]

    for s in range(strips):
        screened[:, s * broad : (s + 1) * broad] = dot(waves_ref[:, :half], screen[s]).astype(BF16)

    groups = NVC // LANES
    scale = 1.0 / math.sqrt(NVC) / math.sqrt(NG)
    source = lax.broadcasted_iota(jnp.int32, (LANES, LANES), 0)
    target = lax.broadcasted_iota(jnp.int32, (LANES, LANES), 1)
    weave = jnp.where(target == source % NV * repeat + source // NV, 1.0, 0.0).astype(BF16)

    cores, _, _, share, places = shares.shape

    def put(kind, i, value):
        to, at = i * LANES // places, i * LANES % places
        for b in range(count // share):
            strip, core = b // cores, b % cores
            shares[core, to * strips + strip, kind, :, at : at + LANES] = value[b * share : (b + 1) * share]

    for kind in range(2):
        raw = dot_rows(conduction[...], screened[...]).astype(BF16) if kind == 0 else raw.T
        for j in range(NC):
            for g in range(groups):
                slabs[kind, g * NC : (g + 1) * NC, j * LANES : (j + 1) * LANES] = raw[
                    j * NC : (j + 1) * NC, g * LANES : (g + 1) * LANES
                ]
        total = dot(slabs[kind], diagonal[kind]) * scale
        if kind == 0:
            for g in range(groups):
                block = total[g * NC : (g + 1) * NC, :]
                stacked = jnp.concatenate([block[:, r * count : (r + 1) * count] for r in range(repeat)], axis=0)
                put(0, g, stacked.T.astype(BF16))
            continue
        for t in range(lanes // LANES):
            sides[t] = total[:, t * LANES : (t + 1) * LANES]
        for at in range(0, groups, fold):
            strands = []
            for r in range(repeat):
                for w in range(repeat):
                    pieces = [
                        sides[r // fold, pl.ds((at + f) * repeat + w, groups, stride=NV), :][
                            :, r % fold * count : (r % fold + 1) * count
                        ]
                        for f in range(fold)
                    ]
                    strands.append(jnp.concatenate(pieces, axis=1))
            stacked = jnp.concatenate(strands, axis=0).astype(BF16)
            woven = lax.dot_general(stacked, weave, (((0,), (0,)), ((), ())), preferred_element_type=F32)
            for f in range(fold):
                put(1, at + f, woven[f * count : (f + 1) * count].astype(BF16))
    keep_ref[...] = shares[side]
    give_ref[...] = shares[1 - side]


def add_kernel(one_ref, other_ref, out_ref):
    out_ref[...] = (one_ref[...].astype(F32) + other_ref[...].astype(F32)).astype(BF16)


def gather_kernel(kpts_ref, got_ref, out_ref):
    out_ref[...] = jnp.zeros_like(out_ref)
    halves, low, strips = got_ref.shape[:3]
    for p in range(low * strips):
        for s in range(2):
            total = got_ref[0, p // strips, p % strips, s].astype(F32)
            for h in range(1, halves):
                total += got_ref[h, p // strips, p % strips, s].astype(F32)
            out_ref[kpts_ref[s, p]] += total


def on_device(orbitals, screening, trial, pair_kpts, pair_q):
    halves, low, strips, groups = (lax.axis_size(a) for a in ("ph", "pl", "bx", "bc"))
    pair_axes = ("ph", "pl")
    pair_count = halves * low
    points, kpt_count, _ = orbitals.shape
    states, _, count = trial.shape
    tall, kinds, broad = screening.shape
    half = NG // HALVES
    aligned = points % LANES == 0 and states % LANES == 0 and pair_count & (pair_count - 1) == 0
    orbital_t, trial_t = orbitals.transpose(1, 2, 0), trial.transpose(1, 2, 0)
    kpts_t = pair_kpts.T

    if aligned:
        send, *screen_sends = call(
            pack_kernel,
            [
                ("s", kpts_t),
                ("s", pair_q),
                ("h", orbital_t),
                ("h", trial_t),
                ("h", screening.reshape(tall * kinds, broad)),
            ],
            [("h", (pair_count, count, points + states), BF16)] + [("b", (tall, broad), BF16)] * (low * strips),
            [
                pltpu.VMEM((low, count, points + states), BF16),
                pltpu.VMEM((tall * kinds, broad), BF16),
                pltpu.VMEM((broad // LANES, tall * kinds, LANES), F32),
                pltpu.SemaphoreType.DMA((low, 3)),
                pltpu.SemaphoreType.DMA((halves, low)),
                pltpu.SemaphoreType.DMA,
            ],
            flops=NG * NG * 256,
        )
    else:
        bx, bc = lax.axis_index("bx"), lax.axis_index("bc")
        near = lax.dynamic_index_in_dim(pair_kpts.reshape(low, strips, 2), bx, 1, keepdims=False)
        orbital_half = lax.dynamic_slice_in_dim(orbital_t, bc * NV, NV, 1)
        orbital_part = orbital_half[near].reshape(low, 2 * NV, points)
        trial_part = trial_t[lax.dynamic_index_in_dim(near, bc, 1, keepdims=False)]
        send = jnp.concatenate([orbital_part, trial_part], axis=2)
        send = jnp.concatenate([send] * halves, axis=0)
        screen_send = screening.transpose(1, 0, 2)[pair_q]
    got = lax.all_to_all(send, pair_axes, split_axis=0, concat_axis=0, tiled=True)
    basis = call(
        basis_kernel,
        [],
        [("v", (NR // 2, 2 * half), BF16)],
        [pltpu.VMEM((TABLE, 2 * half), F32)] * 4,
        flops=NR * NG * 8,
    )[0]
    if aligned:
        screens = list(screen_sends[:1])
        for step, distance in list(enumerate(distances(low * strips)))[1:]:
            to = [
                (i * groups + g, (i ^ distance[g % 2]) * groups + g) for i in range(low * strips) for g in range(groups)
            ]
            screens.append(lax.ppermute(screen_sends[step], ("pl", "bx", "bc"), to))
    else:
        screen_got = lax.all_to_all(screen_send, ("pl", "bx"), split_axis=0, concat_axis=0, tiled=True)
    other = lax.ppermute(got, "bc", [(i, i ^ 1) for i in range(groups)])

    if not aligned:

        def joined(x):
            turned = x.transpose(1, 0, 2)
            return jnp.concatenate(
                [turned[:, :, :points].reshape(1, count, NR), turned[:, :, points:].reshape(1, count, NVC)], axis=2
            )

        got, other = joined(got), joined(other)
        screen_got = screen_got.reshape(low, strips, tall // 2, 2, broad // 2, 2).transpose(1, 3, 0, 2, 5, 4)
        screens = [screen_got.reshape(strips, low * tall, broad)]

    share = count // (strips * groups)
    lanes = LANES // NV * count
    places = states if aligned else NVC
    shape = (NVC // places * strips, 2, share, places)
    waves = call(
        waves_kernel,
        [("v", got), ("v", other), ("v", basis)],
        [("v", (NR // 2, 2 * half), BF16)],
        [pltpu.VMEM((2, 2, NV, NR // 2), F32)] * 2 + [pltpu.VMEM((2, NVC, NR // 2), BF16)] * 2,
        flops=2 * NVC * NR * half,
        aliases={2: 0},
    )[0]
    keep, give = call(
        pair_kernel,
        [("v", got), ("v", other), ("v", waves)] + [("v", x) for x in screens],
        [("v", shape, BF16)] * 2,
        [
            pltpu.VMEM((NVC, half), BF16),
            pltpu.VMEM((strips, half, broad), BF16),
            pltpu.VMEM((NVC, half), BF16),
            pltpu.VMEM((2, NVC // LANES * NC, NC * LANES), BF16),
            pltpu.VMEM((2, NVC, LANES), F32),
            pltpu.VMEM((2, NC * LANES, lanes), BF16),
            pltpu.VMEM((lanes // LANES, NVC // LANES * NC, LANES), F32),
            pltpu.VMEM((groups,) + shape, BF16),
        ],
        flops=2 * NVC * half * half + 8 * NVC * NVC * half,
    )
    taken = lax.ppermute(give, "bc", [(i, i ^ 1) for i in range(groups)])
    partial = call(add_kernel, [("v", keep), ("v", taken)], [("v", shape, BF16)])[0]
    if not aligned:
        partial = partial.reshape(strips, 2, share, pair_count, states).transpose(3, 0, 1, 2, 4)
        partial = partial.reshape(pair_count * strips, 2, share, states)
    out_got = lax.all_to_all(partial, ("ph", "pl", "bx"), split_axis=0, concat_axis=0, tiled=True)
    out_got = out_got.reshape(halves, low, strips, 2, share, states)
    if aligned:
        applied = call(gather_kernel, [("s", kpts_t), ("v", out_got)], [("b", (kpt_count, share, states), F32)])[0]
    else:
        summed = jnp.sum(out_got.astype(F32), axis=0).reshape(-1, share * states)
        hot = (pair_kpts.reshape(-1)[None, :] == jnp.arange(kpt_count)[:, None]).astype(F32)
        applied = lax.dot_general(
            hot, summed, (((1,), (0,)), ((), ())), precision=lax.Precision.HIGHEST, preferred_element_type=F32
        ).reshape(kpt_count, share, states)
    return applied.transpose(2, 0, 1)


def solution(mesh):
    pair_count, band_count = mesh.shape["pair"], mesh.shape["band"]
    shape = (HALVES, pair_count // HALVES, 2, band_count // 2)
    fine = Mesh(mesh.devices.reshape(shape), ("ph", "pl", "bx", "bc"))
    pair_axes, band_axes = ("ph", "pl"), ("bx", "bc")
    return jax.shard_map(
        on_device,
        mesh=fine,
        in_specs=(
            P(pair_axes, None, None),
            P(pair_axes, None, band_axes),
            P(pair_axes, None, None),
            P(),
            P(),
        ),
        out_specs=P(pair_axes, None, band_axes),
        check_vma=False,
    )
```

```python
import functools
import math

import jax
import jax.numpy as jnp
from jax import lax
from jax.experimental import pallas as pl
from jax.experimental.pallas import tpu as pltpu
from jax.sharding import Mesh, PartitionSpec as P


NV = 32
NC = 32
NR = 2048
NG = 1024
NVC = NV * NC
LANES = 128
HALVES = 2
TABLE = 32
F32 = jnp.float32
BF16 = jnp.bfloat16
VMEM_LIMIT = 40 * 1024 * 1024


def dot(a, b):
    return lax.dot_general(a, b, (((1,), (0,)), ((), ())), preferred_element_type=F32)


def dot_rows(a, b):
    return lax.dot_general(a, b, (((1,), (1,)), ((), ())), preferred_element_type=F32)


SPACES = {"s": pltpu.SMEM, "m": pltpu.SMEM, "v": pltpu.VMEM, "h": pl.ANY}


def call(body, inputs, outputs, scratch=(), flops=0, aliases=None):
    specs, arrays = [], []
    for space, array in inputs:
        specs.append(pl.BlockSpec(memory_space=SPACES.get(space, pltpu.VMEM)))
        home = {"v": pltpu.VMEM, "m": pltpu.SMEM}.get(space, pltpu.HBM)
        array = pltpu.with_memory_space_constraint(array, home)
        arrays.append(array)
    shapes, out_specs = [], []
    for space, shape, dtype in outputs:
        kind = {"v": pltpu.VMEM, "h": pltpu.HBM}.get(space, jax.ShapeDtypeStruct)
        shapes.append(kind(shape, dtype))
        out_specs.append(pl.BlockSpec(memory_space=SPACES.get(space, pltpu.VMEM)))
    return pl.pallas_call(
        body,
        out_shape=shapes,
        in_specs=specs,
        out_specs=out_specs,
        scratch_shapes=list(scratch),
        input_output_aliases=aliases or {},
        compiler_params=pltpu.CompilerParams(vmem_limit_bytes=VMEM_LIMIT),
        cost_estimate=pl.CostEstimate(flops=int(flops), transcendentals=0, bytes_accessed=1 << 20),
    )(*arrays)


def pack_kernel(kpts_ref, q_ref, orbital_ref, trial_ref, screen_ref, out_ref, *refs):
    *sends, basis_ref, room, table, ordered, cos_low, sin_low, cos_high, sin_high = refs[:-3]
    fetch_sems, send_sems, table_sem = refs[-3:]
    bx, bc = lax.axis_index("bx"), lax.axis_index("bc")
    strips, low = lax.axis_size("bx"), room.shape[0]
    points = orbital_ref.shape[2]
    bands = pl.ds(pl.multiple_of(bc * NV, NV), NV)
    fetches = []
    for d in range(low):
        pair = d * strips + bx
        first, second, own = kpts_ref[0, pair], kpts_ref[1, pair], kpts_ref[bc, pair]
        parts = (
            (orbital_ref.at[first, bands, :], room.at[d, pl.ds(0, NV), pl.ds(0, points)]),
            (orbital_ref.at[second, bands, :], room.at[d, pl.ds(NV, NV), pl.ds(0, points)]),
            (trial_ref.at[own], room.at[d, :, pl.ds(points, trial_ref.shape[2])]),
        )
        fetches.append([pltpu.make_async_copy(x, y, fetch_sems.at[d, k]) for k, (x, y) in enumerate(parts)])
        for fetch in fetches[-1]:
            fetch.start()
    table_fetch = pltpu.make_async_copy(screen_ref, table, table_sem)
    table_fetch.start()
    basis_tables(cos_low, sin_low, cos_high, sin_high)
    basis_rows(basis_ref, cos_low, sin_low, cos_high, sin_high)
    copies = []
    for d in range(low):
        for fetch in fetches[d]:
            fetch.wait()
        for h in range(out_ref.shape[0] // low):
            copies.append(pltpu.make_async_copy(room.at[d], out_ref.at[h * low + d], send_sems.at[h, d]))
            copies[-1].start()
    table_fetch.wait()
    me = lax.axis_index(("pl", "bx"))
    rows, columns = sends[0].shape
    kinds = screen_ref.shape[0] // rows
    source = lax.broadcasted_iota(jnp.int32, (columns, columns), 0)
    target = lax.broadcasted_iota(jnp.int32, (columns, columns), 1)
    wanted = target % (columns // 2) * 2 + target // (columns // 2)
    order = jnp.where(source == wanted, 1.0, 0.0).astype(BF16)
    result = dot(table[...], order)
    for t in range(columns // LANES):
        ordered[t] = result[:, t * LANES : (t + 1) * LANES]
    for distance, send in zip(distances(len(sends)), sends):
        q = q_ref[me ^ own_distance(distance)]
        for odd in range(2):
            for t in range(columns // LANES):
                send[odd * rows // 2 : (odd + 1) * rows // 2, t * LANES : (t + 1) * LANES] = ordered[
                    t, pl.ds(q + kinds * odd, rows // 2, stride=2 * kinds), :
                ].astype(BF16)
    for copy in copies:
        copy.wait()


def basis_kernel(basis_ref, *tables):
    basis_tables(*tables)
    basis_rows(basis_ref, *tables)


def basis_tables(cos_low, sin_low, cos_high, sin_high):
    columns = cos_low.shape[1]
    quarter = columns // 4
    groups = lax.axis_size("bc")
    strip = NG // (lax.axis_size("bx") * groups)
    column = lax.broadcasted_iota(jnp.int32, (1, columns), 1)
    odd = column // quarter % 2
    inner = column % quarter
    frequency = jnp.where(
        column < 2 * quarter,
        lax.axis_index("ph") * 2 * quarter + 2 * inner,
        (inner // (strip // 2) * groups + lax.axis_index("bc")) * strip + 2 * (inner % (strip // 2)),
    ) + odd
    period = 4 * NR
    unit = math.pi / (2 * NR)
    fine = 8

    def turn(count, step, offset):
        multiple = lax.broadcasted_iota(jnp.int32, (count, columns), 0) * step + offset
        index = multiple * frequency & (period - 1)
        angle = jnp.where(index >= period // 2, index - period, index).astype(F32) * unit
        return jnp.cos(angle), jnp.sin(angle)

    def table(step, offset, cos_ref, sin_ref, scale):
        cos_a, sin_a = turn(fine, step, offset)
        cos_b, sin_b = turn(TABLE // fine, step * fine, 0)
        cos_a, sin_a = cos_a * scale, sin_a * scale
        for k in range(TABLE // fine):
            c, s = cos_b[k : k + 1], sin_b[k : k + 1]
            cos_ref[k * fine : (k + 1) * fine, :] = cos_a * c - sin_a * s
            sin_ref[k * fine : (k + 1) * fine, :] = sin_a * c + cos_a * s

    table(2, 1, cos_low, sin_low, math.sqrt(2.0 / NR))
    table(2 * TABLE, 0, cos_high, sin_high, 1.0)


def basis_rows(basis_ref, cos_low, sin_low, cos_high, sin_high):
    half = basis_ref.shape[2]

    def step(block, carry):
        high = pl.ds(block, 1)
        value = (cos_low[...] * cos_high[high, :] - sin_low[...] * sin_high[high, :]).astype(BF16)
        rows = pl.ds(pl.multiple_of(block * TABLE, TABLE), TABLE)
        for kind in range(2):
            basis_ref[kind, rows, :] = value[:, kind * half : (kind + 1) * half]
        return carry

    lax.fori_loop(0, basis_ref.shape[1] // TABLE, step, 0)


def distances(count):
    order = [0] + [d for d in (1, 7, 5, 3, 6, 4, 2) if d < count]
    order += [d for d in range(1, count) if d not in order]
    return [(d, (d << 1) % count | (d << 1) // count) for d in order]


def own_distance(pair):
    return jnp.where(lax.axis_index("bc") % 2 == 0, pair[0], pair[1])


def waves_kernel(own, orbital_ref, _, waves_ref, sets, even, odd):
    side = lax.axis_index("bc")
    kind = side if own else 1 - side
    blocks, _, _ = orbital_ref.shape
    points = NR // blocks
    piece = 256 if points % 256 == 0 else LANES
    middle = NR // 2
    quarter = waves_ref.shape[2] // 2
    source = lax.broadcasted_iota(jnp.int32, (piece, piece), 0)
    target = lax.broadcasted_iota(jnp.int32, (piece, piece), 1)
    flip = jnp.where(source + target == piece - 1, 1.0, 0.0).astype(BF16)
    for start in range(0, middle, piece):
        ahead = orbital_ref[start // points, :, start % points : start % points + piece].astype(F32)
        mirror = NR - start - piece
        behind = dot(orbital_ref[mirror // points, :, mirror % points : mirror % points + piece], flip)
        for half_of, value in enumerate((ahead, behind)):
            sets[kind, half_of, :, start : start + piece] = value[:NV]
            sets[1 - kind, half_of, :, start : start + piece] = value[NV:]
    for v in range(NV):
        rows = slice(v * NV, (v + 1) * NV)
        ahead = sets[0, 0, v : v + 1, :] * sets[1, 0]
        behind = sets[0, 1, v : v + 1, :] * sets[1, 1]
        even[rows, :] = (ahead + behind).astype(BF16)
        odd[rows, :] = (ahead - behind).astype(BF16)
    spans = (slice(0, quarter), slice(quarter, 2 * quarter))
    results = [dot(x[...], waves_ref[kind, :, span]).astype(BF16) for x, span in zip((even, odd), spans)]
    for span, result in zip(spans, results):
        waves_ref[kind, :, span] = result


def pair_kernel(own_ref, other_ref, waves_ref, *refs):
    *screens, keep_ref, give_ref, conduction, screen, screened = refs[:-5]
    slabs, vectors, diagonal, sides, shares = refs[-5:]
    side = lax.axis_index("bc")
    blocks, count, width = own_ref.shape
    states = NVC // blocks
    half = screened.shape[1]
    quarter = half // 2
    strips = lax.axis_size("bx")
    run = quarter // strips
    broad = screen.shape[2]
    for parity in range(2):
        for s in range(strips):
            source, target = parity * quarter + s * run, (2 * s + parity) * run
            conduction[:, target : target + run] = waves_ref[1, :, source : source + run]
    if len(screens) > 1:
        me = lax.axis_index(("pl", "bx"))
        part = screens[0].shape[0] // 2
        for distance, ref in zip(distances(len(screens)), screens):
            origin = me ^ own_distance(distance)
            for parity in range(2):
                at = pl.multiple_of(parity * quarter + origin // strips * part, part)
                screen[origin % strips, pl.ds(at, part), :] = ref[parity * part : (parity + 1) * part, :]
    else:
        screen[...] = screens[0][...]

    repeat = LANES // NV
    lanes = repeat * count
    fold = LANES // count
    lane = lax.broadcasted_iota(jnp.int32, (NV, lanes), 1) // count
    masks = [jnp.where(lane == r, 1.0, 0.0).astype(BF16) for r in range(repeat)]
    for b in range(blocks):
        for slot, ref in ((side, own_ref), (1 - side, other_ref)):
            turned = ref[b, :, width - states :].astype(F32).T
            vectors[slot, b * states : (b + 1) * states, :] = jnp.concatenate([turned] * fold, axis=1)
    for kind in range(2):
        for j in range(NC):
            rows = vectors[1, pl.ds(j, NV, stride=NV), :] if kind == 0 else vectors[0, j * NC : (j + 1) * NC, :]
            rows = jnp.concatenate([rows.astype(BF16)] * (lanes // LANES), axis=1)
            for r in range(repeat):
                diagonal[kind, j * LANES + r * NV : j * LANES + (r + 1) * NV, :] = rows * masks[r]

    for s in range(strips):
        screened[:, s * broad : (s + 1) * broad] = dot(waves_ref[0], screen[s]).astype(BF16)

    groups = NVC // LANES
    scale = 1.0 / math.sqrt(NVC) / math.sqrt(NG)
    source = lax.broadcasted_iota(jnp.int32, (LANES, LANES), 0)
    target = lax.broadcasted_iota(jnp.int32, (LANES, LANES), 1)
    weave = jnp.where(target == source % NV * repeat + source // NV, 1.0, 0.0).astype(BF16)

    cores, _, _, share, places = shares.shape

    def put(kind, i, value):
        to, at = i * LANES // places, i * LANES % places
        for b in range(count // share):
            strip, core = b // cores, b % cores
            shares[core, to * strips + strip, kind, :, at : at + LANES] = value[b * share : (b + 1) * share]

    for kind in range(2):
        raw = dot_rows(conduction[...], screened[...]).astype(BF16) if kind == 0 else raw.T
        for j in range(NC):
            for g in range(groups):
                slabs[kind, g * NC : (g + 1) * NC, j * LANES : (j + 1) * LANES] = raw[
                    j * NC : (j + 1) * NC, g * LANES : (g + 1) * LANES
                ]
        total = dot(slabs[kind], diagonal[kind]) * scale
        if kind == 0:
            for g in range(groups):
                block = total[g * NC : (g + 1) * NC, :]
                stacked = jnp.concatenate([block[:, r * count : (r + 1) * count] for r in range(repeat)], axis=0)
                put(0, g, stacked.T.astype(BF16))
            continue
        for t in range(lanes // LANES):
            sides[t] = total[:, t * LANES : (t + 1) * LANES]
        for at in range(0, groups, fold):
            strands = []
            for r in range(repeat):
                for w in range(repeat):
                    pieces = [
                        sides[r // fold, pl.ds((at + f) * repeat + w, groups, stride=NV), :][
                            :, r % fold * count : (r % fold + 1) * count
                        ]
                        for f in range(fold)
                    ]
                    strands.append(jnp.concatenate(pieces, axis=1))
            stacked = jnp.concatenate(strands, axis=0).astype(BF16)
            woven = lax.dot_general(stacked, weave, (((0,), (0,)), ((), ())), preferred_element_type=F32)
            for f in range(fold):
                put(1, at + f, woven[f * count : (f + 1) * count].astype(BF16))
    keep_ref[...] = shares[side]
    give_ref[...] = shares[1 - side]


def add_kernel(one_ref, other_ref, out_ref):
    out_ref[...] = (one_ref[...].astype(F32) + other_ref[...].astype(F32)).astype(BF16)


def gather_kernel(kpts_ref, got_ref, out_ref):
    out_ref[...] = jnp.zeros_like(out_ref)
    halves, low, strips = got_ref.shape[:3]
    for p in range(low * strips):
        for s in range(2):
            total = got_ref[0, p // strips, p % strips, s].astype(F32)
            for h in range(1, halves):
                total += got_ref[h, p // strips, p % strips, s].astype(F32)
            out_ref[kpts_ref[s, p]] += total


def on_device(orbitals, screening, trial, pair_kpts, pair_q):
    halves, low, strips, groups = (lax.axis_size(a) for a in ("ph", "pl", "bx", "bc"))
    pair_axes = ("ph", "pl")
    pair_count = halves * low
    points, kpt_count, _ = orbitals.shape
    states, _, count = trial.shape
    tall, kinds, broad = screening.shape
    half = NG // HALVES
    aligned = points % LANES == 0 and states % LANES == 0 and pair_count & (pair_count - 1) == 0
    orbital_t, trial_t = orbitals.transpose(1, 2, 0), trial.transpose(1, 2, 0)
    kpts_t = pair_kpts.T
    basis_out = [("v", (2, NR // 2, half), BF16)]
    tables = [pltpu.VMEM((TABLE, 2 * half), F32)] * 4

    if aligned:
        send, *screen_sends, basis = call(
            pack_kernel,
            [
                ("s", kpts_t),
                ("s", pair_q),
                ("h", orbital_t),
                ("h", trial_t),
                ("h", screening.reshape(tall * kinds, broad)),
            ],
            [("h", (pair_count, count, points + states), BF16)] + [("b", (tall, broad), BF16)] * (low * strips) + basis_out,
            [
                pltpu.VMEM((low, count, points + states), BF16),
                pltpu.VMEM((tall * kinds, broad), BF16),
                pltpu.VMEM((broad // LANES, tall * kinds, LANES), F32),
                *tables,
                pltpu.SemaphoreType.DMA((low, 3)),
                pltpu.SemaphoreType.DMA((halves, low)),
                pltpu.SemaphoreType.DMA,
            ],
            flops=NG * NG * 256,
        )
    else:
        bx, bc = lax.axis_index("bx"), lax.axis_index("bc")
        near = lax.dynamic_index_in_dim(pair_kpts.reshape(low, strips, 2), bx, 1, keepdims=False)
        orbital_half = lax.dynamic_slice_in_dim(orbital_t, bc * NV, NV, 1)
        orbital_part = orbital_half[near].reshape(low, 2 * NV, points)
        trial_part = trial_t[lax.dynamic_index_in_dim(near, bc, 1, keepdims=False)]
        send = jnp.concatenate([orbital_part, trial_part], axis=2)
        send = jnp.concatenate([send] * halves, axis=0)
        basis = call(basis_kernel, [], basis_out, tables, flops=NR * NG)[0]
        screen_send = screening.transpose(1, 0, 2)[pair_q]
    got = lax.all_to_all(send, pair_axes, split_axis=0, concat_axis=0, tiled=True)
    if aligned:
        screens = list(screen_sends[:1])
        for step, distance in list(enumerate(distances(low * strips)))[1:]:
            to = [
                (i * groups + g, (i ^ distance[g % 2]) * groups + g) for i in range(low * strips) for g in range(groups)
            ]
            screens.append(lax.ppermute(screen_sends[step], ("pl", "bx", "bc"), to))
    else:
        screen_got = lax.all_to_all(screen_send, ("pl", "bx"), split_axis=0, concat_axis=0, tiled=True)
    other = lax.ppermute(got, "bc", [(i, i ^ 1) for i in range(groups)])

    if not aligned:

        def joined(x):
            turned = x.transpose(1, 0, 2)
            return jnp.concatenate(
                [turned[:, :, :points].reshape(1, count, NR), turned[:, :, points:].reshape(1, count, NVC)], axis=2
            )

        got, other = joined(got), joined(other)
        screen_got = screen_got.reshape(low, strips, tall // 2, 2, broad // 2, 2).transpose(1, 3, 0, 2, 5, 4)
        screens = [screen_got.reshape(strips, low * tall, broad)]

    share = count // (strips * groups)
    lanes = LANES // NV * count
    places = states if aligned else NVC
    shape = (NVC // places * strips, 2, share, places)
    waves = basis
    for own, half_of_bands in ((True, got), (False, other)):
        waves = call(
            functools.partial(waves_kernel, own),
            [("v", half_of_bands), ("v", waves)],
            basis_out,
            [pltpu.VMEM((2, 2, NV, NR // 2), F32)] + [pltpu.VMEM((NVC, NR // 2), BF16)] * 2,
            flops=NVC * NR * half,
            aliases={1: 0},
        )[0]
    keep, give = call(
        pair_kernel,
        [("v", got), ("v", other), ("v", waves)] + [("v", x) for x in screens],
        [("v", shape, BF16)] * 2,
        [
            pltpu.VMEM((NVC, half), BF16),
            pltpu.VMEM((strips, half, broad), BF16),
            pltpu.VMEM((NVC, half), BF16),
            pltpu.VMEM((2, NVC // LANES * NC, NC * LANES), BF16),
            pltpu.VMEM((2, NVC, LANES), F32),
            pltpu.VMEM((2, NC * LANES, lanes), BF16),
            pltpu.VMEM((lanes // LANES, NVC // LANES * NC, LANES), F32),
            pltpu.VMEM((groups,) + shape, BF16),
        ],
        flops=2 * NVC * half * half + 8 * NVC * NVC * half,
    )
    taken = lax.ppermute(give, "bc", [(i, i ^ 1) for i in range(groups)])
    partial = call(add_kernel, [("v", keep), ("v", taken)], [("v", shape, BF16)])[0]
    if not aligned:
        partial = partial.reshape(strips, 2, share, pair_count, states).transpose(3, 0, 1, 2, 4)
        partial = partial.reshape(pair_count * strips, 2, share, states)
    out_got = lax.all_to_all(partial, ("ph", "pl", "bx"), split_axis=0, concat_axis=0, tiled=True)
    out_got = out_got.reshape(halves, low, strips, 2, share, states)
    if aligned:
        applied = call(gather_kernel, [("m", kpts_t), ("v", out_got)], [("b", (kpt_count, share, states), F32)])[0]
    else:
        summed = jnp.sum(out_got.astype(F32), axis=0).reshape(-1, share * states)
        hot = (pair_kpts.reshape(-1)[None, :] == jnp.arange(kpt_count)[:, None]).astype(F32)
        applied = lax.dot_general(
            hot, summed, (((1,), (0,)), ((), ())), precision=lax.Precision.HIGHEST, preferred_element_type=F32
        ).reshape(kpt_count, share, states)
    return applied.transpose(2, 0, 1)


def solution(mesh):
    pair_count, band_count = mesh.shape["pair"], mesh.shape["band"]
    shape = (HALVES, pair_count // HALVES, 2, band_count // 2)
    fine = Mesh(mesh.devices.reshape(shape), ("ph", "pl", "bx", "bc"))
    pair_axes, band_axes = ("ph", "pl"), ("bx", "bc")
    return jax.shard_map(
        on_device,
        mesh=fine,
        in_specs=(
            P(pair_axes, None, None),
            P(pair_axes, None, band_axes),
            P(pair_axes, None, None),
            P(),
            P(),
        ),
        out_specs=P(pair_axes, None, band_axes),
        check_vma=False,
    )
```

```python
import functools
import math

import jax
import jax.numpy as jnp
from jax import lax
from jax.experimental import pallas as pl
from jax.experimental.pallas import tpu as pltpu
from jax.sharding import Mesh, PartitionSpec as P


NV = 32
NC = 32
NR = 2048
NG = 1024
NVC = NV * NC
LANES = 128
HALVES = 2
TABLE = 32
F32 = jnp.float32
BF16 = jnp.bfloat16
VMEM_LIMIT = 40 * 1024 * 1024


def dot(a, b):
    return lax.dot_general(a, b, (((1,), (0,)), ((), ())), preferred_element_type=F32)


def dot_rows(a, b):
    return lax.dot_general(a, b, (((1,), (1,)), ((), ())), preferred_element_type=F32)


SPACES = {"s": pltpu.SMEM, "m": pltpu.SMEM, "v": pltpu.VMEM, "h": pl.ANY}


def call(body, inputs, outputs, scratch=(), flops=0, aliases=None):
    specs, arrays = [], []
    for space, array in inputs:
        specs.append(pl.BlockSpec(memory_space=SPACES.get(space, pltpu.VMEM)))
        home = {"v": pltpu.VMEM, "m": pltpu.SMEM}.get(space, pltpu.HBM)
        array = pltpu.with_memory_space_constraint(array, home)
        arrays.append(array)
    shapes, out_specs = [], []
    for space, shape, dtype in outputs:
        kind = {"v": pltpu.VMEM, "h": pltpu.HBM}.get(space, jax.ShapeDtypeStruct)
        shapes.append(kind(shape, dtype))
        out_specs.append(pl.BlockSpec(memory_space=SPACES.get(space, pltpu.VMEM)))
    return pl.pallas_call(
        body,
        out_shape=shapes,
        in_specs=specs,
        out_specs=out_specs,
        scratch_shapes=list(scratch),
        input_output_aliases=aliases or {},
        compiler_params=pltpu.CompilerParams(vmem_limit_bytes=VMEM_LIMIT),
        cost_estimate=pl.CostEstimate(flops=int(flops), transcendentals=0, bytes_accessed=1 << 20),
    )(*arrays)


def pack_kernel(kpts_ref, q_ref, orbital_ref, trial_ref, screen_ref, out_ref, *refs):
    *sends, basis_ref, room, table, ordered, cos_low, sin_low, cos_high, sin_high = refs[:-3]
    fetch_sems, send_sems, table_sem = refs[-3:]
    bx, bc = lax.axis_index("bx"), lax.axis_index("bc")
    strips, low = lax.axis_size("bx"), room.shape[0]
    points = orbital_ref.shape[2]
    bands = pl.ds(pl.multiple_of(bc * NV, NV), NV)
    fetches = []
    for d in range(low):
        pair = d * strips + bx
        first, second, own = kpts_ref[0, pair], kpts_ref[1, pair], kpts_ref[bc, pair]
        parts = (
            (orbital_ref.at[first, bands, :], room.at[d, pl.ds(0, NV), pl.ds(0, points)]),
            (orbital_ref.at[second, bands, :], room.at[d, pl.ds(NV, NV), pl.ds(0, points)]),
            (trial_ref.at[own], room.at[d, :, pl.ds(points, trial_ref.shape[2])]),
        )
        fetches.append([pltpu.make_async_copy(x, y, fetch_sems.at[d, k]) for k, (x, y) in enumerate(parts)])
        for fetch in fetches[-1]:
            fetch.start()
    table_fetch = pltpu.make_async_copy(screen_ref, table, table_sem)
    table_fetch.start()
    basis_tables(cos_low, sin_low, cos_high, sin_high)
    basis_rows(basis_ref, cos_low, sin_low, cos_high, sin_high)
    copies = []
    for d in range(low):
        for fetch in fetches[d]:
            fetch.wait()
        for h in range(out_ref.shape[0] // low):
            copies.append(pltpu.make_async_copy(room.at[d], out_ref.at[h * low + d], send_sems.at[h, d]))
            copies[-1].start()
    table_fetch.wait()
    me = lax.axis_index(("pl", "bx"))
    rows, columns = sends[0].shape
    kinds = screen_ref.shape[0] // rows
    source = lax.broadcasted_iota(jnp.int32, (columns, columns), 0)
    target = lax.broadcasted_iota(jnp.int32, (columns, columns), 1)
    wanted = target % (columns // 2) * 2 + target // (columns // 2)
    order = jnp.where(source == wanted, 1.0, 0.0).astype(BF16)
    result = dot(table[...], order)
    for t in range(columns // LANES):
        ordered[t] = result[:, t * LANES : (t + 1) * LANES]
    for distance, send in zip(distances(len(sends)), sends):
        q = q_ref[me ^ own_distance(distance)]
        for odd in range(2):
            for t in range(columns // LANES):
                send[odd * rows // 2 : (odd + 1) * rows // 2, t * LANES : (t + 1) * LANES] = ordered[
                    t, pl.ds(q + kinds * odd, rows // 2, stride=2 * kinds), :
                ].astype(BF16)
    for copy in copies:
        copy.wait()


def basis_kernel(basis_ref, *tables):
    basis_tables(*tables)
    basis_rows(basis_ref, *tables)


def basis_tables(cos_low, sin_low, cos_high, sin_high):
    columns = cos_low.shape[1]
    quarter = columns // 4
    groups = lax.axis_size("bc")
    strip = NG // (lax.axis_size("bx") * groups)
    column = lax.broadcasted_iota(jnp.int32, (1, columns), 1)
    odd = column // quarter % 2
    inner = column % quarter
    frequency = jnp.where(
        column < 2 * quarter,
        lax.axis_index("ph") * 2 * quarter + 2 * inner,
        (inner // (strip // 2) * groups + lax.axis_index("bc")) * strip + 2 * (inner % (strip // 2)),
    ) + odd
    period = 4 * NR
    unit = math.pi / (2 * NR)
    fine = 8

    def turn(count, step, offset):
        multiple = lax.broadcasted_iota(jnp.int32, (count, columns), 0) * step + offset
        index = multiple * frequency & (period - 1)
        angle = jnp.where(index >= period // 2, index - period, index).astype(F32) * unit
        return jnp.cos(angle), jnp.sin(angle)

    def table(step, offset, cos_ref, sin_ref, scale):
        cos_a, sin_a = turn(fine, step, offset)
        cos_b, sin_b = turn(TABLE // fine, step * fine, 0)
        cos_a, sin_a = cos_a * scale, sin_a * scale
        for k in range(TABLE // fine):
            c, s = cos_b[k : k + 1], sin_b[k : k + 1]
            cos_ref[k * fine : (k + 1) * fine, :] = cos_a * c - sin_a * s
            sin_ref[k * fine : (k + 1) * fine, :] = sin_a * c + cos_a * s

    table(2, 1, cos_low, sin_low, math.sqrt(2.0 / NR))
    table(2 * TABLE, 0, cos_high, sin_high, 1.0)


def basis_rows(basis_ref, cos_low, sin_low, cos_high, sin_high):
    half = basis_ref.shape[2]

    def step(block, carry):
        high = pl.ds(block, 1)
        value = (cos_low[...] * cos_high[high, :] - sin_low[...] * sin_high[high, :]).astype(BF16)
        rows = pl.ds(pl.multiple_of(block * TABLE, TABLE), TABLE)
        for kind in range(2):
            basis_ref[kind, rows, :] = value[:, kind * half : (kind + 1) * half]
        return carry

    lax.fori_loop(0, basis_ref.shape[1] // TABLE, step, 0, unroll=True)


def distances(count):
    order = [0] + [d for d in (7, 5, 6, 4, 3, 1, 2) if d < count]
    order += [d for d in range(1, count) if d not in order]
    return [(d, (d << 1) % count | (d << 1) // count) for d in order]


def own_distance(pair):
    return jnp.where(lax.axis_index("bc") % 2 == 0, pair[0], pair[1])


def waves_kernel(own, orbital_ref, _, waves_ref, sets, even, odd):
    side = lax.axis_index("bc")
    kind = side if own else 1 - side
    blocks, _, _ = orbital_ref.shape
    points = NR // blocks
    piece = 256 if points % 256 == 0 else LANES
    middle = NR // 2
    quarter = waves_ref.shape[2] // 2
    source = lax.broadcasted_iota(jnp.int32, (piece, piece), 0)
    target = lax.broadcasted_iota(jnp.int32, (piece, piece), 1)
    flip = jnp.where(source + target == piece - 1, 1.0, 0.0).astype(BF16)
    for start in range(0, middle, piece):
        ahead = orbital_ref[start // points, :, start % points : start % points + piece].astype(F32)
        mirror = NR - start - piece
        behind = dot(orbital_ref[mirror // points, :, mirror % points : mirror % points + piece], flip)
        for half_of, value in enumerate((ahead, behind)):
            sets[kind, half_of, :, start : start + piece] = value[:NV]
            sets[1 - kind, half_of, :, start : start + piece] = value[NV:]
    for v in range(NV):
        rows = slice(v * NV, (v + 1) * NV)
        ahead = sets[0, 0, v : v + 1, :] * sets[1, 0]
        behind = sets[0, 1, v : v + 1, :] * sets[1, 1]
        even[rows, :] = (ahead + behind).astype(BF16)
        odd[rows, :] = (ahead - behind).astype(BF16)
    spans = (slice(0, quarter), slice(quarter, 2 * quarter))
    results = [dot(x[...], waves_ref[kind, :, span]).astype(BF16) for x, span in zip((even, odd), spans)]
    for span, result in zip(spans, results):
        waves_ref[kind, :, span] = result


def pair_kernel(own_ref, other_ref, waves_ref, *refs):
    *screens, keep_ref, give_ref, conduction, screen, screened = refs[:-5]
    slabs, vectors, diagonal, sides, shares = refs[-5:]
    side = lax.axis_index("bc")
    blocks, count, width = own_ref.shape
    states = NVC // blocks
    half = screened.shape[1]
    quarter = half // 2
    strips = lax.axis_size("bx")
    run = quarter // strips
    broad = screen.shape[2]
    for parity in range(2):
        for s in range(strips):
            source, target = parity * quarter + s * run, (2 * s + parity) * run
            conduction[:, target : target + run] = waves_ref[1, :, source : source + run]
    if len(screens) > 1:
        me = lax.axis_index(("pl", "bx"))
        part = screens[0].shape[0] // 2
        for distance, ref in zip(distances(len(screens)), screens):
            origin = me ^ own_distance(distance)
            for parity in range(2):
                at = pl.multiple_of(parity * quarter + origin // strips * part, part)
                screen[origin % strips, pl.ds(at, part), :] = ref[parity * part : (parity + 1) * part, :]
    else:
        screen[...] = screens[0][...]

    repeat = LANES // NV
    lanes = repeat * count
    fold = LANES // count
    lane = lax.broadcasted_iota(jnp.int32, (NV, lanes), 1) // count
    masks = [jnp.where(lane == r, 1.0, 0.0).astype(BF16) for r in range(repeat)]
    for b in range(blocks):
        for slot, ref in ((side, own_ref), (1 - side, other_ref)):
            turned = ref[b, :, width - states :].astype(F32).T
            vectors[slot, b * states : (b + 1) * states, :] = jnp.concatenate([turned] * fold, axis=1)
    for kind in range(2):
        for j in range(NC):
            rows = vectors[1, pl.ds(j, NV, stride=NV), :] if kind == 0 else vectors[0, j * NC : (j + 1) * NC, :]
            rows = jnp.concatenate([rows.astype(BF16)] * (lanes // LANES), axis=1)
            for r in range(repeat):
                diagonal[kind, j * LANES + r * NV : j * LANES + (r + 1) * NV, :] = rows * masks[r]

    for s in range(strips):
        screened[:, s * broad : (s + 1) * broad] = dot(waves_ref[0], screen[s]).astype(BF16)

    groups = NVC // LANES
    scale = 1.0 / math.sqrt(NVC) / math.sqrt(NG)
    source = lax.broadcasted_iota(jnp.int32, (LANES, LANES), 0)
    target = lax.broadcasted_iota(jnp.int32, (LANES, LANES), 1)
    weave = jnp.where(target == source % NV * repeat + source // NV, 1.0, 0.0).astype(BF16)

    cores, _, _, share, places = shares.shape

    def put(kind, i, value):
        to, at = i * LANES // places, i * LANES % places
        for b in range(count // share):
            strip, core = b // cores, b % cores
            shares[core, to * strips + strip, kind, :, at : at + LANES] = value[b * share : (b + 1) * share]

    for kind in range(2):
        raw = dot_rows(conduction[...], screened[...]).astype(BF16) if kind == 0 else raw.T
        for j in range(NC):
            for g in range(groups):
                slabs[kind, g * NC : (g + 1) * NC, j * LANES : (j + 1) * LANES] = raw[
                    j * NC : (j + 1) * NC, g * LANES : (g + 1) * LANES
                ]
        total = dot(slabs[kind], diagonal[kind]) * scale
        if kind == 0:
            for g in range(groups):
                block = total[g * NC : (g + 1) * NC, :]
                stacked = jnp.concatenate([block[:, r * count : (r + 1) * count] for r in range(repeat)], axis=0)
                put(0, g, stacked.T.astype(BF16))
            continue
        for t in range(lanes // LANES):
            sides[t] = total[:, t * LANES : (t + 1) * LANES]
        for at in range(0, groups, fold):
            strands = []
            for r in range(repeat):
                for w in range(repeat):
                    pieces = [
                        sides[r // fold, pl.ds((at + f) * repeat + w, groups, stride=NV), :][
                            :, r % fold * count : (r % fold + 1) * count
                        ]
                        for f in range(fold)
                    ]
                    strands.append(jnp.concatenate(pieces, axis=1))
            stacked = jnp.concatenate(strands, axis=0).astype(BF16)
            woven = lax.dot_general(stacked, weave, (((0,), (0,)), ((), ())), preferred_element_type=F32)
            for f in range(fold):
                put(1, at + f, woven[f * count : (f + 1) * count].astype(BF16))
    keep_ref[...] = shares[side]
    give_ref[...] = shares[1 - side]


def gather_kernel(kpts_ref, got_ref, out_ref):
    out_ref[...] = jnp.zeros_like(out_ref)
    halves, low, strips = got_ref.shape[:3]
    for p in range(low * strips):
        for s in range(2):
            total = got_ref[0, p // strips, p % strips, s].astype(F32)
            for h in range(1, halves):
                total += got_ref[h, p // strips, p % strips, s].astype(F32)
            out_ref[kpts_ref[s, p]] += total


def on_device(orbitals, screening, trial, pair_kpts, pair_q):
    halves, low, strips, groups = (lax.axis_size(a) for a in ("ph", "pl", "bx", "bc"))
    pair_axes = ("ph", "pl")
    pair_count = halves * low
    points, kpt_count, _ = orbitals.shape
    states, _, count = trial.shape
    tall, kinds, broad = screening.shape
    half = NG // HALVES
    aligned = points % LANES == 0 and states % LANES == 0 and pair_count & (pair_count - 1) == 0
    orbital_t, trial_t = orbitals.transpose(1, 2, 0), trial.transpose(1, 2, 0)
    kpts_t = pair_kpts.T
    basis_out = [("v", (2, NR // 2, half), BF16)]
    tables = [pltpu.VMEM((TABLE, 2 * half), F32)] * 4

    if aligned:
        send, *screen_sends, basis = call(
            pack_kernel,
            [
                ("s", kpts_t),
                ("s", pair_q),
                ("h", orbital_t),
                ("h", trial_t),
                ("h", screening.reshape(tall * kinds, broad)),
            ],
            [("h", (pair_count, count, points + states), BF16)] + [("b", (tall, broad), BF16)] * (low * strips) + basis_out,
            [
                pltpu.VMEM((low, count, points + states), BF16),
                pltpu.VMEM((tall * kinds, broad), BF16),
                pltpu.VMEM((broad // LANES, tall * kinds, LANES), F32),
                *tables,
                pltpu.SemaphoreType.DMA((low, 3)),
                pltpu.SemaphoreType.DMA((halves, low)),
                pltpu.SemaphoreType.DMA,
            ],
            flops=NG * NG * 256,
        )
    else:
        bx, bc = lax.axis_index("bx"), lax.axis_index("bc")
        near = lax.dynamic_index_in_dim(pair_kpts.reshape(low, strips, 2), bx, 1, keepdims=False)
        orbital_half = lax.dynamic_slice_in_dim(orbital_t, bc * NV, NV, 1)
        orbital_part = orbital_half[near].reshape(low, 2 * NV, points)
        trial_part = trial_t[lax.dynamic_index_in_dim(near, bc, 1, keepdims=False)]
        send = jnp.concatenate([orbital_part, trial_part], axis=2)
        send = jnp.concatenate([send] * halves, axis=0)
        basis = call(basis_kernel, [], basis_out, tables, flops=NR * NG)[0]
        screen_send = screening.transpose(1, 0, 2)[pair_q]
    got = lax.all_to_all(send, pair_axes, split_axis=0, concat_axis=0, tiled=True)
    if aligned:
        screens = list(screen_sends[:1])
        for step, distance in list(enumerate(distances(low * strips)))[1:]:
            to = [
                (i * groups + g, (i ^ distance[g % 2]) * groups + g) for i in range(low * strips) for g in range(groups)
            ]
            screens.append(lax.ppermute(screen_sends[step], ("pl", "bx", "bc"), to))
    else:
        screen_got = lax.all_to_all(screen_send, ("pl", "bx"), split_axis=0, concat_axis=0, tiled=True)
    other = lax.ppermute(got, "bc", [(i, i ^ 1) for i in range(groups)])

    if not aligned:

        def joined(x):
            turned = x.transpose(1, 0, 2)
            return jnp.concatenate(
                [turned[:, :, :points].reshape(1, count, NR), turned[:, :, points:].reshape(1, count, NVC)], axis=2
            )

        got, other = joined(got), joined(other)
        screen_got = screen_got.reshape(low, strips, tall // 2, 2, broad // 2, 2).transpose(1, 3, 0, 2, 5, 4)
        screens = [screen_got.reshape(strips, low * tall, broad)]

    share = count // (strips * groups)
    lanes = LANES // NV * count
    places = states if aligned else NVC
    shape = (NVC // places * strips, 2, share, places)
    waves = basis
    for own, half_of_bands in ((True, got), (False, other)):
        waves = call(
            functools.partial(waves_kernel, own),
            [("v", half_of_bands), ("v", waves)],
            basis_out,
            [pltpu.VMEM((2, 2, NV, NR // 2), F32)] + [pltpu.VMEM((NVC, NR // 2), BF16)] * 2,
            flops=NVC * NR * half,
            aliases={1: 0},
        )[0]
    keep, give = call(
        pair_kernel,
        [("v", got), ("v", other), ("v", waves)] + [("v", x) for x in screens],
        [("v", shape, BF16)] * 2,
        [
            pltpu.VMEM((NVC, half), BF16),
            pltpu.VMEM((strips, half, broad), BF16),
            pltpu.VMEM((NVC, half), BF16),
            pltpu.VMEM((2, NVC // LANES * NC, NC * LANES), BF16),
            pltpu.VMEM((2, NVC, LANES), F32),
            pltpu.VMEM((2, NC * LANES, lanes), BF16),
            pltpu.VMEM((lanes // LANES, NVC // LANES * NC, LANES), F32),
            pltpu.VMEM((groups,) + shape, BF16),
        ],
        flops=2 * NVC * half * half + 8 * NVC * NVC * half,
    )
    taken = lax.ppermute(give, "bc", [(i, i ^ 1) for i in range(groups)])
    partial = (keep.astype(F32) + taken.astype(F32)).astype(BF16)
    if not aligned:
        partial = partial.reshape(strips, 2, share, pair_count, states).transpose(3, 0, 1, 2, 4)
        partial = partial.reshape(pair_count * strips, 2, share, states)
    out_got = lax.all_to_all(partial, ("ph", "pl", "bx"), split_axis=0, concat_axis=0, tiled=True)
    out_got = out_got.reshape(halves, low, strips, 2, share, states)
    if aligned:
        applied = call(gather_kernel, [("m", kpts_t), ("v", out_got)], [("b", (kpt_count, share, states), F32)])[0]
    else:
        summed = jnp.sum(out_got.astype(F32), axis=0).reshape(-1, share * states)
        hot = (pair_kpts.reshape(-1)[None, :] == jnp.arange(kpt_count)[:, None]).astype(F32)
        applied = lax.dot_general(
            hot, summed, (((1,), (0,)), ((), ())), precision=lax.Precision.HIGHEST, preferred_element_type=F32
        ).reshape(kpt_count, share, states)
    return applied.transpose(2, 0, 1)


def solution(mesh):
    pair_count, band_count = mesh.shape["pair"], mesh.shape["band"]
    shape = (HALVES, pair_count // HALVES, 2, band_count // 2)
    fine = Mesh(mesh.devices.reshape(shape), ("ph", "pl", "bx", "bc"))
    pair_axes, band_axes = ("ph", "pl"), ("bx", "bc")
    return jax.shard_map(
        on_device,
        mesh=fine,
        in_specs=(
            P(pair_axes, None, None),
            P(pair_axes, None, band_axes),
            P(pair_axes, None, None),
            P(),
            P(),
        ),
        out_specs=P(pair_axes, None, band_axes),
        check_vma=False,
    )
```
